256 devices in a mesh: fsdp: 8 (over y, core), expert: 32 (over x, z).
Axes of the slice: x: 4, y: 4, z: 8, core: 2. Of those that a mesh axis runs over, the one named last changes fastest.
Arguments:
- tokens: bfloat16 [32768, 1024], P(('fsdp', 'expert')), may hold values from -6 to 6
- expert_ids: int32 [32768, 2], P(('fsdp', 'expert')), may hold values from 0 to 31, all different within a row; in each aligned block of 128 rows (0 to 127, 128 to 255, ...) at most 16 rows name the same one
- gate_weights: float32 [32768, 2], P(('fsdp', 'expert')), may hold values from 0.2 to 1
- weight_in: bfloat16 [32, 2048, 1024], P('expert', 'fsdp'), may hold values from -0.1875 to 0.1875
- weight_out: bfloat16 [32, 2048, 1024], P('expert', 'fsdp'), may hold values from -0.125 to 0.125
- cotangent: bfloat16 [32768, 1024], P(('fsdp', 'expert')), may hold values from -3 to 3
Outputs:
- layer_out: bfloat16 [32768, 1024], P(('fsdp', 'expert'))
- token_grad: bfloat16 [32768, 1024], P(('fsdp', 'expert'))
- grad_in: float32 [32, 2048, 1024], P('expert', 'fsdp')
- grad_out: float32 [32, 2048, 1024], P('expert', 'fsdp')
The draws below stay inside these ranges and needn't reach their ends.
Inputs may be any that keep to these rules, and one draw needn't show every extreme that they name: `expert_ids`: the two experts of a token differ. Among the 128 tokens of one device no expert is chosen by more than 16 tokens, and some device has an expert chosen by exactly 16 tokens.
All inputs are finite; a program needn't handle non-finite values.
Results may differ from the reference program's by a relative error of at most 0.014.
Values may be sent and summed in bfloat16 or wider, within the bound.
No kernel may reach another device: no remote copies, remote signals or barrier semaphores. Data moves between devices by JAX's collectives and lax.ppermute only.
A program may use at most 128 MiB of HBM per device.

```python
import math
import jax
import jax.numpy as jnp
import numpy as np
from jax import lax

D = 1024
HID = 2048
TOK_DEV = 128
EXPERTS = 32
CAP = 16
TOKENS = 32768
N_FSDP = 8


def level_of(own_key, dims, cuts, smallest, largest):
    factor_of = 1.0
    for dim, parts in cuts:
        steps = jax.random.uniform(jax.random.fold_in(jax.random.fold_in(own_key, 6), dim), (parts,), jnp.float32, smallest / len(cuts), largest / len(cuts))
        factor_of = factor_of * jnp.repeat(jnp.exp(steps), dims[dim] // parts).reshape((-1,) + (1,) * (len(dims) - 1 - dim))
    return factor_of


def deal_out(own_key, own, number, rows, number_of, top, limit, lean):
    order = jax.random.permutation(own_key, number_of)
    packed, ordinary = portions_of(number_of, rows * top, limit, lean, True), portions_of(number_of, rows * top, limit, lean, False)
    places = jnp.arange(number_of)

    def named(lengths, turn):
        used = int((lengths > 0).sum())
        fixed = max(1, used // 4)
        shifted = fixed + (places - fixed + turn * (used - fixed)) % max(1, number_of - fixed)
        return jnp.zeros((number_of,), jnp.int32).at[order[jnp.where(places < fixed, places, shifted)]].set(jnp.asarray(lengths, jnp.int32))

    lengths = jnp.where(number % 4 == 0, named(packed, number // 4), named(ordinary, number - number // 4 - 1))
    mixed = jax.random.permutation(jax.random.fold_in(own, 3), number_of)
    donor, sink = mixed[0:number_of // 2 * 2:2], mixed[1:number_of // 2 * 2:2]
    slack = jnp.minimum(lengths[donor] - 1, limit - lengths[sink]) // 2
    slack = jnp.where((donor == order[0]) | (sink == order[0]) | (lengths[sink] == 0), 0, jnp.maximum(slack, 0))
    shifted = jax.random.randint(jax.random.fold_in(own, 4), (number_of // 2,), 0, 1 << 20) % (slack + 1)
    lengths = lengths.at[donor].add(-shifted).at[sink].add(shifted)
    items = jnp.searchsorted(jnp.cumsum(lengths), jnp.arange(rows * top), side="right").astype(jnp.int32)
    listing = items.reshape(top, rows).T
    listing = listing[jax.random.permutation(jax.random.fold_in(own, 1), rows)]
    turn = jax.random.randint(jax.random.fold_in(own, 2), (rows, 1), 0, top)
    return jnp.take_along_axis(listing, (jnp.arange(top)[None, :] + turn) % top, axis=1)


def portions_of(amount, total, bound, lean, full):
    portions = [(1 << 20) // math.isqrt(rank ** lean) + 1 for rank in range(1, amount + 1)]
    largest = bound if full else min(bound, max(-(-total // amount), total * portions[0] // sum(portions)))
    least = 1 if total - largest >= amount - 1 else 0
    given, surplus = [largest] + [least] * (amount - 1), total - largest - least * (amount - 1)
    while surplus > 0:
        candidates = [i for i in range(1, amount) if given[i] < largest] or [i for i in range(1, amount) if given[i] < bound]
        mass, remaining = sum([portions[i] for i in candidates]), surplus
        for i in candidates:
            extra = min(bound - given[i], max(1, remaining * portions[i] // mass), surplus)
            given[i] = given[i] + extra
            surplus = surplus - extra
    return np.array(given)


def centred(stream_key, shape, scale, most, shards=(), kind=jnp.bfloat16):
    entries = scale * jax.random.normal(stream_key, shape, jnp.float32)
    if shards:
        entries = entries * level_of(stream_key, shape, shards, -0.22, 0.18)
    return jnp.clip(entries, -most, most).astype(kind)


def setup_inputs(seed: int = 0) -> dict:
    keys = jax.random.split(jax.random.key(seed), 7)
    tokens = centred(keys[0], (TOKENS, D), 1.0, 6.0, ((0, 256),))
    expert_ids_keys = jax.random.split(jax.random.fold_in(keys[1], 1), TOKENS // TOK_DEV)
    expert_ids_turns = jax.random.permutation(jax.random.fold_in(keys[1], 3), TOKENS // TOK_DEV)
    expert_ids = jax.vmap(lambda own, number: deal_out(jax.random.fold_in(keys[1], 2), own, number, TOK_DEV, EXPERTS, 2, CAP, 1))(expert_ids_keys, expert_ids_turns).reshape((TOKENS, 2))
    gate_weights = jnp.clip(0.2 + 0.8 * jax.random.uniform(keys[2], (TOKENS, 2), jnp.float32) ** level_of(keys[2], (TOKENS, 2), ((0, 256),), -0.2, 0.2), 0.2, 1.0)
    weight_in = centred(keys[3], (EXPERTS, HID, D), D ** -0.5, 0.1875, ((0, 32), (1, 8)))
    weight_out = centred(keys[4], (EXPERTS, HID, D), HID ** -0.5, 0.125, ((0, 32), (1, 8)))
    cotangent = centred(keys[5], (TOKENS, D), 0.5, 3.0, ((0, 256),))
    return dict(tokens=tokens, expert_ids=expert_ids, gate_weights=gate_weights, weight_in=weight_in, weight_out=weight_out, cotangent=cotangent)


def gelu_back(pre_act, upstream):
    _, pullback = jax.vjp(jax.nn.gelu, pre_act)
    return pullback(upstream)[0]

def reference(tokens, expert_ids, gate_weights, weight_in, weight_out, cotangent):
    groups = TOKENS // TOK_DEV
    per_group = expert_ids.reshape(groups, TOK_DEV, 2)
    labels = jnp.arange(EXPERTS, dtype=jnp.int32)
    hit_count = lax.optimization_barrier(jnp.sum((per_group[:, :, :, None] == labels).astype(jnp.int32), axis=2, dtype=jnp.int32))
    earlier = jnp.cumsum(hit_count, axis=1, dtype=jnp.int32) - hit_count
    slot_ids = jnp.take_along_axis(earlier, per_group, axis=2).astype(jnp.int32)
    group_ids = jnp.broadcast_to(jnp.arange(groups, dtype=jnp.int32)[:, None, None], per_group.shape)
    token_ids = jnp.broadcast_to(jnp.arange(TOKENS, dtype=jnp.int32).reshape(groups, TOK_DEV, 1), per_group.shape)
    table = jnp.zeros((EXPERTS, groups, CAP), jnp.int32).at[per_group, group_ids, slot_ids].set(token_ids)
    filled = jnp.zeros((EXPERTS, groups, CAP), jnp.float32).at[per_group, group_ids, slot_ids].set(1.0)
    gate_table = jnp.zeros((EXPERTS, groups, CAP), jnp.float32).at[per_group, group_ids, slot_ids].set(gate_weights.reshape(groups, TOK_DEV, 2))

    def one_expert(index):
        where_rows = table[index].reshape(-1)
        live = filled[index].reshape(-1, 1)
        expert_rows = jnp.where(live > 0, tokens[where_rows], jnp.zeros((), jnp.bfloat16))
        activation = jnp.dot(expert_rows, weight_in[index].T, preferred_element_type=jnp.float32)
        hidden = jax.nn.gelu(activation).astype(jnp.bfloat16)
        stored = activation.astype(jnp.bfloat16)
        expert_out = jnp.dot(hidden, weight_out[index], preferred_element_type=jnp.float32).astype(jnp.bfloat16)
        grad_rows = (cotangent[where_rows].astype(jnp.float32) * gate_table[index].reshape(-1, 1)).astype(jnp.bfloat16)
        grad_hidden = jnp.dot(grad_rows, weight_out[index].T, preferred_element_type=jnp.float32)
        grad_act = gelu_back(stored.astype(jnp.float32), grad_hidden).astype(jnp.bfloat16)
        grad_rows_in = jnp.dot(grad_act, weight_in[index], preferred_element_type=jnp.float32).astype(jnp.bfloat16)
        rows_split = expert_rows.reshape(N_FSDP, -1, D).astype(jnp.float32)
        act_split = grad_act.reshape(N_FSDP, -1, HID).astype(jnp.float32)
        hid_split = hidden.reshape(N_FSDP, -1, HID).astype(jnp.float32)
        grad_split = grad_rows.reshape(N_FSDP, -1, D).astype(jnp.float32)
        part_in = jnp.einsum('frh,frd->fhd', act_split, rows_split, precision=lax.Precision.HIGHEST)
        part_out = jnp.einsum('frh,frd->fhd', hid_split, grad_split, precision=lax.Precision.HIGHEST)
        part_in = lax.optimization_barrier(part_in.astype(jnp.bfloat16)).astype(jnp.float32).sum(0)
        part_out = lax.optimization_barrier(part_out.astype(jnp.bfloat16)).astype(jnp.float32).sum(0)
        return (expert_out, grad_rows_in, part_in, part_out)
    expert_out, grad_rows_in, grad_in, grad_out = lax.map(one_expert, jnp.arange(EXPERTS, dtype=jnp.int32))
    flat_index = (per_group * (groups * CAP) + group_ids * CAP + slot_ids).reshape(TOKENS, 2)
    picked = expert_out.reshape(-1, D)[flat_index].astype(jnp.float32)
    layer_out = lax.optimization_barrier(jnp.sum(picked * gate_weights[:, :, None], axis=1)).astype(jnp.bfloat16)
    picked_grad = grad_rows_in.reshape(-1, D)[flat_index].astype(jnp.float32)
    token_grad = lax.optimization_barrier(jnp.sum(picked_grad, axis=1)).astype(jnp.bfloat16)
    return (layer_out, token_grad, grad_in, grad_out)
```

```python
import functools

import jax
import jax.numpy as jnp
from jax import lax
from jax.experimental import pallas as pl
from jax.experimental.pallas import tpu as pltpu
from jax.sharding import PartitionSpec as P


PAIR_A = [(2 * y + c, 2 * (y ^ 1) + c) for y in range(4) for c in range(2)]
PAIR_B = [(2 * y + c, 2 * (3 - y) + c) for y in range(4) for c in range(2)]
PAIR_C = [(f, f ^ 1) for f in range(8)]
F32 = jnp.float32
BF16 = jnp.bfloat16


def place_kernel(
    experts, ids_hbm, gate_hbm, tok_hbm, cells_ref, place_ref, hi_ref, lo_ref, ids_ref, gate_ref, tok_ref, sems
):
    copies = [
        pltpu.make_async_copy(a, b, sems.at[i])
        for i, (a, b) in enumerate([(ids_hbm, ids_ref), (gate_hbm, gate_ref), (tok_hbm, tok_ref)])
    ]
    for copy in copies:
        copy.start()
    copies[0].wait()
    cells, n = place_ref.shape
    capacity = cells // experts
    ids0, ids1 = ids_ref[0:1, :], ids_ref[1:2, :]
    label = lax.broadcasted_iota(jnp.int32, (experts, n), 0)
    oh0, oh1 = ids0 == label, ids1 == label
    hit = jnp.where(oh0 | oh1, 1.0, 0.0).astype(BF16)
    before = lax.broadcasted_iota(jnp.int32, (n, n), 0) < lax.broadcasted_iota(jnp.int32, (n, n), 1)
    earlier = jnp.dot(hit, jnp.where(before, 1.0, 0.0).astype(BF16), preferred_element_type=F32)
    slot0 = jnp.sum(jnp.where(oh0, earlier, 0.0), axis=0, keepdims=True).astype(jnp.int32)
    slot1 = jnp.sum(jnp.where(oh1, earlier, 0.0), axis=0, keepdims=True).astype(jnp.int32)
    cell = lax.broadcasted_iota(jnp.int32, (cells, n), 0)
    at0 = cell == ids0 * capacity + slot0
    at1 = cell == ids1 * capacity + slot1
    place = jnp.where(at0 | at1, 1.0, 0.0).astype(BF16)
    place_ref[...] = place
    copies[1].wait()
    gate = jnp.where(at0, gate_ref[0:1, :], 0.0) + jnp.where(at1, gate_ref[1:2, :], 0.0)
    hi = gate.astype(BF16)
    hi_ref[...] = hi
    lo_ref[...] = (gate - hi.astype(F32)).astype(BF16)
    copies[2].wait()
    cells_ref[...] = jnp.dot(place, tok_ref[...], preferred_element_type=F32).astype(BF16)


def scatter_kernel(hi_ref, lo_ref, cot_ref, cells_ref):
    cot = cot_ref[...]
    cells_ref[...] = (
        jnp.dot(hi_ref[...], cot, preferred_element_type=F32)
        + jnp.dot(lo_ref[...], cot, preferred_element_type=F32)
    ).astype(BF16)


def gated_kernel(hi_ref, lo_ref, rows_ref, out_ref):
    rows = rows_ref[...]
    out_ref[...] = (dot_0(hi_ref[...], rows) + dot_0(lo_ref[...], rows)).astype(BF16)


def plain_kernel(place_ref, rows_ref, out_ref):
    out_ref[...] = dot_0(place_ref[...], rows_ref[...]).astype(BF16)


def call(kernel, outs, *args, flops=3e8):
    shapes = [jax.ShapeDtypeStruct(s, d) for s, d in outs]
    return pl.pallas_call(
        kernel,
        out_shape=shapes if len(shapes) > 1 else shapes[0],
        in_specs=[pl.BlockSpec(memory_space=pltpu.VMEM)] * len(args),
        out_specs=[pl.BlockSpec(memory_space=pltpu.VMEM)] * len(shapes)
        if len(shapes) > 1
        else pl.BlockSpec(memory_space=pltpu.VMEM),
        cost_estimate=pl.CostEstimate(flops=int(flops), bytes_accessed=3 << 20, transcendentals=0),
        compiler_params=pltpu.CompilerParams(vmem_limit_bytes=16 << 20),
    )(*args)


def gelu_back(pre_act, upstream):
    _, pullback = jax.vjp(jax.nn.gelu, pre_act)
    return pullback(upstream)[0]


def dot_t(a, b):
    return lax.dot_general(a, b, (((1,), (1,)), ((), ())), preferred_element_type=F32)


def dot_0(a, b):
    return lax.dot_general(a, b, (((0,), (0,)), ((), ())), preferred_element_type=F32)


def exchange(rows, experts):
    count, width = rows.shape
    return lax.all_to_all(
        rows.reshape(experts, count // experts, width),
        "expert",
        split_axis=0,
        concat_axis=0,
        tiled=True,
    ).reshape(count, width)


def permute(x, pairs):
    return lax.ppermute(x, "fsdp", pairs)


def gather(shard, first, second):
    got = permute(shard, first)
    two = jnp.concatenate([shard, got], axis=0)
    other = permute(two, second)
    core_two = permute(two, PAIR_C)
    core_other = permute(other, PAIR_C)
    return two, other, core_two, core_other


def layer(tokens, expert_ids, gate_weights, weight_in, weight_out, cotangent):
    n, width = tokens.shape
    experts = lax.axis_size("expert")
    cells = 4 * n
    unit = weight_in.shape[1]
    in_a, in_b, in_ca, in_cb = gather(weight_in[0], PAIR_A, PAIR_B)
    out_a, out_b, out_ca, out_cb = gather(weight_out[0], PAIR_B, PAIR_A)

    tok_cells, place, hi, lo = pl.pallas_call(
        functools.partial(place_kernel, experts),
        out_shape=[jax.ShapeDtypeStruct((cells, width), BF16)] + [jax.ShapeDtypeStruct((cells, n), BF16)] * 3,
        in_specs=[pl.BlockSpec(memory_space=pl.ANY)] * 3,
        out_specs=[pl.BlockSpec(memory_space=pltpu.VMEM)] * 4,
        scratch_shapes=[
            pltpu.VMEM((2, n), jnp.int32),
            pltpu.VMEM((2, n), F32),
            pltpu.VMEM(tokens.shape, BF16),
            pltpu.SemaphoreType.DMA((3,)),
        ],
        cost_estimate=pl.CostEstimate(flops=1 << 28, bytes_accessed=3 << 20, transcendentals=0),
        compiler_params=pltpu.CompilerParams(vmem_limit_bytes=16 << 20),
    )(expert_ids.T, gate_weights.T, tokens)
    rows = exchange(tok_cells, experts)
    cot_cells = call(scatter_kernel, [((cells, width), BF16)], hi, lo, cotangent)
    grad_rows = exchange(cot_cells, experts)

    full_in = jnp.concatenate([in_a, in_b, in_ca, in_cb], axis=0)
    full_out = jnp.concatenate(
        [
            out_a[:unit],
            out_b[:unit],
            out_a[unit:],
            out_b[unit:],
            out_ca[:unit],
            out_cb[:unit],
            out_ca[unit:],
            out_cb[unit:],
        ],
        axis=0,
    )
    activation = dot_t(rows, full_in)
    hidden = jax.nn.gelu(activation).astype(BF16)
    stored = activation.astype(BF16)
    expert_out = jnp.dot(hidden, full_out, preferred_element_type=F32).astype(BF16)
    returned = exchange(expert_out, experts)

    half = 4 * unit
    part_out = dot_0(hidden, grad_rows)
    got = permute(part_out[half:].astype(BF16), PAIR_C)
    sum_out = part_out[:half] + got.astype(F32)
    grad_hidden = dot_t(grad_rows, full_out)
    grad_act = gelu_back(stored.astype(F32), grad_hidden).astype(BF16)
    part_in = dot_0(grad_act, rows)
    got = permute(part_in[half:].astype(BF16), PAIR_C)
    sum_in = part_in[:half] + got.astype(F32)
    grad_back = jnp.dot(grad_act, full_in, preferred_element_type=F32).astype(BF16)
    grad_returned = exchange(grad_back, experts)

    sum_in, sum_out = sum_in.astype(BF16), sum_out.astype(BF16)
    got = permute(jnp.concatenate([sum_out[unit : 2 * unit], sum_out[3 * unit :]], axis=0), PAIR_A)
    two_out = (
        jnp.concatenate([sum_out[:unit], sum_out[2 * unit : 3 * unit]], axis=0).astype(F32)
        + got.astype(F32)
    )
    got = permute(two_out[unit:].astype(BF16), PAIR_B)
    grad_out = two_out[:unit] + got.astype(F32)
    got = permute(sum_in[2 * unit :], PAIR_B)
    two_in = sum_in[: 2 * unit].astype(F32) + got.astype(F32)
    got = permute(two_in[unit:].astype(BF16), PAIR_A)
    grad_in = two_in[:unit] + got.astype(F32)

    layer_out = call(gated_kernel, [((n, width), BF16)], hi, lo, returned)
    token_grad = call(plain_kernel, [((n, width), BF16)], place, grad_returned)
    return (layer_out, token_grad, grad_in[None], grad_out[None])


def solution(mesh):
    rows = P(("fsdp", "expert"), None)
    weights = P("expert", "fsdp", None)
    return jax.shard_map(
        layer,
        mesh=mesh,
        in_specs=(rows, rows, rows, weights, weights, rows),
        out_specs=(rows, rows, weights, weights),
        check_vma=False,
    )
```

```python
import functools

import jax
import jax.numpy as jnp
from jax import lax
from jax.experimental import pallas as pl
from jax.experimental.pallas import tpu as pltpu
from jax.sharding import PartitionSpec as P


PAIR_A = [(2 * y + c, 2 * (y ^ 1) + c) for y in range(4) for c in range(2)]
PAIR_B = [(2 * y + c, 2 * (3 - y) + c) for y in range(4) for c in range(2)]
PAIR_C = [(f, f ^ 1) for f in range(8)]
F32 = jnp.float32
BF16 = jnp.bfloat16


def place_kernel(
    experts, ids_hbm, gate_hbm, tok_hbm, cells_ref, place_ref, hi_ref, lo_ref, ids_ref, gate_ref, tok_ref, sems
):
    copies = [
        pltpu.make_async_copy(a, b, sems.at[i])
        for i, (a, b) in enumerate([(ids_hbm, ids_ref), (gate_hbm, gate_ref), (tok_hbm, tok_ref)])
    ]
    for copy in copies:
        copy.start()
    copies[0].wait()
    cells, n = place_ref.shape
    capacity = cells // experts
    ids0, ids1 = ids_ref[0:1, :], ids_ref[1:2, :]
    label = lax.broadcasted_iota(jnp.int32, (experts, n), 0)
    oh0, oh1 = ids0 == label, ids1 == label
    hit = jnp.where(oh0 | oh1, 1.0, 0.0).astype(BF16)
    before = lax.broadcasted_iota(jnp.int32, (n, n), 0) < lax.broadcasted_iota(jnp.int32, (n, n), 1)
    earlier = jnp.dot(hit, jnp.where(before, 1.0, 0.0).astype(BF16), preferred_element_type=F32)
    slot0 = jnp.sum(jnp.where(oh0, earlier, 0.0), axis=0, keepdims=True).astype(jnp.int32)
    slot1 = jnp.sum(jnp.where(oh1, earlier, 0.0), axis=0, keepdims=True).astype(jnp.int32)
    cell = lax.broadcasted_iota(jnp.int32, (cells, n), 0)
    at0 = cell == ids0 * capacity + slot0
    at1 = cell == ids1 * capacity + slot1
    place = jnp.where(at0 | at1, 1.0, 0.0).astype(BF16)
    place_ref[...] = place
    copies[1].wait()
    gate = jnp.where(at0, gate_ref[0:1, :], 0.0) + jnp.where(at1, gate_ref[1:2, :], 0.0)
    hi = gate.astype(BF16)
    hi_ref[...] = hi
    lo_ref[...] = (gate - hi.astype(F32)).astype(BF16)
    copies[2].wait()
    cells_ref[...] = jnp.dot(place, tok_ref[...], preferred_element_type=F32).astype(BF16)


def scatter_kernel(hi_ref, lo_ref, cot_ref, cells_ref):
    cot = cot_ref[...]
    cells_ref[...] = (
        jnp.dot(hi_ref[...], cot, preferred_element_type=F32)
        + jnp.dot(lo_ref[...], cot, preferred_element_type=F32)
    ).astype(BF16)


def gated_kernel(hi_ref, lo_ref, rows_ref, out_ref):
    rows = rows_ref[...]
    out_ref[...] = (dot_0(hi_ref[...], rows) + dot_0(lo_ref[...], rows)).astype(BF16)


def plain_kernel(place_ref, rows_ref, out_ref):
    out_ref[...] = dot_0(place_ref[...], rows_ref[...]).astype(BF16)


def pack_kernel(unit, *refs):
    in_a, in_b, in_ca, in_cb, out_a, out_b, out_ca, out_cb, full_in, full_out, sems = refs
    pieces = []
    for at, (first, second) in enumerate([(in_a, in_b), (in_ca, in_cb)]):
        for place, (ref, row) in enumerate([(first, 0), (first, 1), (second, 1), (second, 0)]):
            pieces.append((ref, row, full_in, 4 * at + place))
    for at, (first, second) in enumerate([(out_a, out_b), (out_ca, out_cb)]):
        for place, (ref, row) in enumerate([(first, 0), (second, 0), (second, 1), (first, 1)]):
            pieces.append((ref, row, full_out, 4 * at + place))
    copies = [
        pltpu.make_async_copy(
            ref.at[pl.ds(row * unit, unit)], full.at[pl.ds(to * unit, unit)], sems.at[i]
        )
        for i, (ref, row, full, to) in enumerate(pieces)
    ]
    for copy in copies:
        copy.start()
    for copy in copies:
        copy.wait()


def finish_kernel(own_l_ref, got_l_ref, own_r_ref, got_r_ref, out_ref):
    half = own_l_ref.shape[1]
    out_ref[:, :half] = own_l_ref[...] + got_l_ref[...].astype(F32)
    out_ref[:, half:] = own_r_ref[...] + got_r_ref[...].astype(F32)


def call(kernel, outs, *args, flops=3e8):
    shapes = [jax.ShapeDtypeStruct(s, d) for s, d in outs]
    return pl.pallas_call(
        kernel,
        out_shape=shapes if len(shapes) > 1 else shapes[0],
        in_specs=[pl.BlockSpec(memory_space=pltpu.VMEM)] * len(args),
        out_specs=[pl.BlockSpec(memory_space=pltpu.VMEM)] * len(shapes)
        if len(shapes) > 1
        else pl.BlockSpec(memory_space=pltpu.VMEM),
        cost_estimate=pl.CostEstimate(flops=int(flops), bytes_accessed=3 << 20, transcendentals=0),
        compiler_params=pltpu.CompilerParams(vmem_limit_bytes=16 << 20),
    )(*args)


def gelu_back(pre_act, upstream):
    _, pullback = jax.vjp(jax.nn.gelu, pre_act)
    return pullback(upstream)[0]


def dot_t(a, b):
    return lax.dot_general(a, b, (((1,), (1,)), ((), ())), preferred_element_type=F32)


def dot_0(a, b):
    return lax.dot_general(a, b, (((0,), (0,)), ((), ())), preferred_element_type=F32)


def exchange(rows, experts):
    count, width = rows.shape
    return lax.all_to_all(
        rows.reshape(experts, count // experts, width),
        "expert",
        split_axis=0,
        concat_axis=0,
        tiled=True,
    ).reshape(count, width)


def permute(x, pairs):
    return lax.ppermute(x, "fsdp", pairs)


def gather(shard, first, second):
    got = permute(shard, first)
    two = jnp.concatenate([shard, got], axis=0)
    other = permute(two, second)
    core_two = permute(two, PAIR_C)
    core_other = permute(other, PAIR_C)
    return two, other, core_two, core_other


def scatter(total, unit):
    half = total.shape[1] // 2
    left, right = total[:, :half], total[:, half:]
    got_l = permute(left[unit : 3 * unit], PAIR_A)
    got_r = permute(right[2 * unit :], PAIR_B)
    own_l = left[:unit].astype(F32) + got_l[:unit].astype(F32)
    next_l = left[3 * unit :].astype(F32) + got_l[unit:].astype(F32)
    own_r = right[:unit].astype(F32) + got_r[unit:].astype(F32)
    next_r = right[unit : 2 * unit].astype(F32) + got_r[:unit].astype(F32)
    got_l = permute(next_l.astype(BF16), PAIR_B)
    got_r = permute(next_r.astype(BF16), PAIR_A)
    return call(finish_kernel, [((unit, 2 * half), F32)], own_l, got_l, own_r, got_r)


def layer(tokens, expert_ids, gate_weights, weight_in, weight_out, cotangent):
    n, width = tokens.shape
    experts = lax.axis_size("expert")
    cells = 4 * n
    unit = weight_in.shape[1]
    in_a, in_b, in_ca, in_cb = gather(weight_in[0], PAIR_A, PAIR_B)
    out_a, out_b, out_ca, out_cb = gather(weight_out[0], PAIR_B, PAIR_A)

    tok_cells, place, hi, lo = pl.pallas_call(
        functools.partial(place_kernel, experts),
        out_shape=[jax.ShapeDtypeStruct((cells, width), BF16)] + [jax.ShapeDtypeStruct((cells, n), BF16)] * 3,
        in_specs=[pl.BlockSpec(memory_space=pltpu.HBM)] * 3,
        out_specs=[pl.BlockSpec(memory_space=pltpu.VMEM)] * 4,
        scratch_shapes=[
            pltpu.VMEM((2, n), jnp.int32),
            pltpu.VMEM((2, n), F32),
            pltpu.VMEM(tokens.shape, BF16),
            pltpu.SemaphoreType.DMA((3,)),
        ],
        cost_estimate=pl.CostEstimate(flops=1 << 28, bytes_accessed=3 << 20, transcendentals=0),
        compiler_params=pltpu.CompilerParams(vmem_limit_bytes=16 << 20),
    )(expert_ids.T, gate_weights.T, tokens)
    rows = exchange(tok_cells, experts)
    cot_cells = call(scatter_kernel, [((cells, width), BF16)], hi, lo, cotangent)
    grad_rows = exchange(cot_cells, experts)

    full_in, full_out = pl.pallas_call(
        functools.partial(pack_kernel, unit),
        out_shape=[jax.ShapeDtypeStruct((8 * unit, width), BF16)] * 2,
        in_specs=[pl.BlockSpec(memory_space=pl.ANY)] * 8,
        out_specs=[pl.BlockSpec(memory_space=pltpu.VMEM)] * 2,
        scratch_shapes=[pltpu.SemaphoreType.DMA((16,))],
        cost_estimate=pl.CostEstimate(flops=0, bytes_accessed=16 << 20, transcendentals=0),
        compiler_params=pltpu.CompilerParams(vmem_limit_bytes=16 << 20),
    )(in_a, in_b, in_ca, in_cb, out_a, out_b, out_ca, out_cb)
    activation = dot_t(rows, full_in)
    hidden = jax.nn.gelu(activation).astype(BF16)
    stored = activation.astype(BF16)
    expert_out = jnp.dot(hidden, full_out, preferred_element_type=F32).astype(BF16)
    returned = exchange(expert_out, experts)

    half = 4 * unit
    part_out = dot_0(hidden, grad_rows)
    got = permute(part_out[half:].astype(BF16), PAIR_C)
    sum_out = part_out[:half] + got.astype(F32)
    grad_hidden = dot_t(grad_rows, full_out)
    grad_act = gelu_back(stored.astype(F32), grad_hidden).astype(BF16)
    part_in = dot_0(grad_act, rows)
    got = permute(part_in[half:].astype(BF16), PAIR_C)
    sum_in = part_in[:half] + got.astype(F32)
    grad_back = jnp.dot(grad_act, full_in, preferred_element_type=F32).astype(BF16)
    grad_returned = exchange(grad_back, experts)

    grad_out = scatter(sum_out.astype(BF16), unit)
    grad_in = scatter(sum_in.astype(BF16), unit)

    layer_out = call(gated_kernel, [((n, width), BF16)], hi, lo, returned)
    token_grad = call(plain_kernel, [((n, width), BF16)], place, grad_returned)
    return (layer_out, token_grad, grad_in[None], grad_out[None])


def solution(mesh):
    rows = P(("fsdp", "expert"), None)
    weights = P("expert", "fsdp", None)
    return jax.shard_map(
        layer,
        mesh=mesh,
        in_specs=(rows, rows, rows, weights, weights, rows),
        out_specs=(rows, rows, weights, weights),
        check_vma=False,
    )
```

```python
import functools

import jax
import jax.numpy as jnp
from jax import lax
from jax.experimental import pallas as pl
from jax.experimental.pallas import tpu as pltpu
from jax.sharding import PartitionSpec as P


PAIR_A = [(2 * y + c, 2 * (y ^ 1) + c) for y in range(4) for c in range(2)]
PAIR_B = [(2 * y + c, 2 * (3 - y) + c) for y in range(4) for c in range(2)]
PAIR_C = [(f, f ^ 1) for f in range(8)]
F32 = jnp.float32
BF16 = jnp.bfloat16
GELU_SCALE = 0.7978845608028654
GELU_CUBIC = 0.044715


def dot_t(a, b):
    return lax.dot_general(a, b, (((1,), (1,)), ((), ())), preferred_element_type=F32)


def dot_0(a, b):
    return lax.dot_general(a, b, (((0,), (0,)), ((), ())), preferred_element_type=F32)


def dot(a, b):
    return jnp.dot(a, b, preferred_element_type=F32)


def cells_of(experts, capacity, ids_ref):
    n = ids_ref.shape[1]
    ids0, ids1 = ids_ref[0:1, :], ids_ref[1:2, :]
    label = lax.broadcasted_iota(jnp.int32, (experts, n), 0)
    oh0, oh1 = ids0 == label, ids1 == label
    hit = jnp.where(oh0 | oh1, 1.0, 0.0).astype(BF16)
    before = lax.broadcasted_iota(jnp.int32, (n, n), 0) < lax.broadcasted_iota(jnp.int32, (n, n), 1)
    earlier = dot(hit, jnp.where(before, 1.0, 0.0).astype(BF16))
    slot0 = jnp.sum(jnp.where(oh0, earlier, 0.0), axis=0, keepdims=True).astype(jnp.int32)
    slot1 = jnp.sum(jnp.where(oh1, earlier, 0.0), axis=0, keepdims=True).astype(jnp.int32)
    cell = lax.broadcasted_iota(jnp.int32, (experts * capacity, n), 0)
    return cell == ids0 * capacity + slot0, cell == ids1 * capacity + slot1


def place_kernel(*refs):
    hbm, out_hbm, local, cells_ref, sems = refs[:4], refs[4], refs[5:9], refs[9], refs[10]
    copies = [pltpu.make_async_copy(a, b, sems.at[i]) for i, (a, b) in enumerate(zip(hbm, local))]
    for copy in copies:
        copy.start()
    ids_ref, gate_ref, tok_ref, cot_ref = local
    experts, slots, width = cells_ref.shape
    capacity = slots // 2
    outs = [
        pltpu.make_async_copy(cells_ref.at[:, part, :], out_hbm.at[:, part, :], sems.at[4 + i])
        for i, part in enumerate((pl.ds(0, capacity), pl.ds(capacity, capacity)))
    ]
    copies[0].wait()
    at0, at1 = cells_of(experts, capacity, ids_ref)
    place = jnp.where(at0 | at1, 1.0, 0.0).astype(BF16)
    copies[2].wait()
    cells_ref[:, :capacity, :] = dot(place, tok_ref[...]).astype(BF16).reshape(experts, capacity, width)
    outs[0].start()
    copies[1].wait()
    gate = jnp.where(at0, gate_ref[0:1, :], 0.0) + jnp.where(at1, gate_ref[1:2, :], 0.0)
    hi = gate.astype(BF16)
    lo = (gate - hi.astype(F32)).astype(BF16)
    copies[3].wait()
    cot = cot_ref[...]
    cells_ref[:, capacity:, :] = (
        (dot(hi, cot) + dot(lo, cot)).astype(BF16).reshape(experts, capacity, width)
    )
    outs[1].start()
    outs[0].wait()
    outs[1].wait()


def weights_kernel(experts, ids_ref, gate_ref, place_ref, hi_ref, lo_ref):
    at0, at1 = cells_of(experts, place_ref.shape[1] // experts, ids_ref)
    place_ref[...] = jnp.transpose(jnp.where(at0 | at1, 1.0, 0.0)).astype(BF16)
    gate = jnp.where(at0, gate_ref[0:1, :], 0.0) + jnp.where(at1, gate_ref[1:2, :], 0.0)
    gate = jnp.transpose(gate)
    hi = gate.astype(BF16)
    hi_ref[...] = hi
    lo_ref[...] = (gate - hi.astype(F32)).astype(BF16)


def expert_kernel(unit, rows_hbm, *refs):
    in_a, in_b, in_ca, in_cb, out_a, out_b, out_ca, out_cb = refs[:8]
    back_hbm, hid_hbm, act_hbm = refs[8:11]
    rows_ref, back_ref, hid_ref, act_ref, full_in, full_out, sems, row_sem, out_sems, back_sems = refs[11:]
    sources, slots, width = rows_ref.shape
    capacity = slots // 2
    count = sources * capacity
    tile = count // 2
    per = sources // 2
    row_copies = [
        pltpu.make_async_copy(
            rows_hbm.at[pl.ds(r * per, per)], rows_ref.at[pl.ds(r * per, per)], row_sem.at[r]
        )
        for r in range(2)
    ]
    order = []
    for first, second, first_out, second_out in [(in_a, in_b, out_a, out_b), (in_ca, in_cb, out_ca, out_cb)]:
        order.append(((first, 0), (first_out, 0)))
        order.append(((first, 1), (second_out, 0)))
        order.append(((second, 1), (second_out, 1)))
        order.append(((second, 0), (first_out, 1)))
    for c, pair in enumerate(order):
        for w, ((ref, row), full) in enumerate(zip(pair, (full_in, full_out))):
            pltpu.make_async_copy(
                ref.at[pl.ds(row * unit, unit)], full.at[pl.ds(c * unit, unit)], sems.at[w, c]
            ).start()
        if c == 0:
            for copy in row_copies:
                copy.start()
    for copy in row_copies:
        copy.wait()

    @pl.loop(0, 8)
    def _(c):
        at = pl.multiple_of(c * unit, unit)
        for w, full in enumerate((full_in, full_out)):
            pltpu.make_async_copy(in_a.at[pl.ds(0, unit)], full.at[pl.ds(at, unit)], sems.at[w, c]).wait()
        w_in, w_out = full_in[pl.ds(at, unit), :], full_out[pl.ds(at, unit), :]
        for r in range(2):
            x = rows_ref[r * per : (r + 1) * per, :capacity, :].reshape(tile, width)
            dy = rows_ref[r * per : (r + 1) * per, capacity:, :].reshape(tile, width)
            pre = dot_t(x, w_in)
            up = dot_t(dy, w_out)
            square = pre * pre
            t = jnp.tanh(GELU_SCALE * pre * (1.0 + GELU_CUBIC * square))
            half = 0.5 * (1.0 + t)
            slope = half + (0.5 * GELU_SCALE) * pre * (1.0 - t * t) * (1.0 + 3.0 * GELU_CUBIC * square)
            hid_ref[r * tile : (r + 1) * tile, pl.ds(at, unit)] = (pre * half).astype(BF16)
            act_ref[r * tile : (r + 1) * tile, pl.ds(at, unit)] = (up * slope).astype(BF16)

    outs = [
        pltpu.make_async_copy(a, b, out_sems.at[i])
        for i, (a, b) in enumerate([(hid_ref, hid_hbm), (act_ref, act_hbm)])
    ]
    for copy in outs:
        copy.start()
    columns = 256

    def back_copy(c, at):
        cut = pl.ds(at, columns)
        return pltpu.make_async_copy(back_ref.at[:, :, cut], back_hbm.at[:, :, cut], back_sems.at[c])

    @pl.loop(0, width // columns)
    def _(c):
        at = pl.multiple_of(c * columns, columns)
        for part, (a_ref, full) in enumerate([(hid_ref, full_out), (act_ref, full_in)]):
            w = full[:, pl.ds(at, columns)]
            for r in range(2):
                got = dot(a_ref[r * tile : (r + 1) * tile, :], w).astype(BF16)
                back_ref[
                    r * per : (r + 1) * per, part * capacity : (part + 1) * capacity, pl.ds(at, columns)
                ] = got.reshape(per, capacity, columns)
        back_copy(c, at).start()

    for c in range(width // columns):
        back_copy(c, c * columns).wait()
    for copy in outs:
        copy.wait()


def grad_kernel(part, unit, acts_ref, rows_ref, keep_ref, send_ref, held_ref):
    _, slots, _ = rows_ref.shape
    capacity = slots // 2
    held_ref[...] = rows_ref[:, part * capacity : (part + 1) * capacity, :].reshape(held_ref.shape)
    for half, ref in ((4, send_ref), (0, keep_ref)):

        @pl.loop(0, 4)
        def _(c):
            at = pl.multiple_of((half + c) * unit, unit)
            got = dot_0(acts_ref[:, pl.ds(at, unit)], held_ref[...]).astype(BF16)
            ref[pl.ds(pl.multiple_of(c * unit, unit), unit), :] = got


def combine_kernel(place_ref, hi_ref, lo_ref, rows_ref, out_ref, grad_ref):
    sources, slots, width = rows_ref.shape
    capacity = slots // 2
    rows = rows_ref[:, :capacity, :].reshape(sources * capacity, width)
    out_ref[...] = (dot(hi_ref[...], rows) + dot(lo_ref[...], rows)).astype(BF16)
    rows = rows_ref[:, capacity:, :].reshape(sources * capacity, width)
    grad_ref[...] = dot(place_ref[...], rows).astype(BF16)


def finish_kernel(own_l_ref, got_l_ref, own_r_ref, got_r_ref, out_ref):
    half = own_l_ref.shape[1]
    out_ref[:, :half] = own_l_ref[...] + got_l_ref[...].astype(F32)
    out_ref[:, half:] = own_r_ref[...] + got_r_ref[...].astype(F32)


def call(kernel, outs, *args, flops=3e8, moved=4 << 20, specs=None, scratch=(), limit=None):
    shapes = [jax.ShapeDtypeStruct(s, d) for s, d in outs]
    vmem = pl.BlockSpec(memory_space=pltpu.VMEM)
    in_specs, out_specs = specs or ([vmem] * len(args), [vmem] * len(shapes))
    single = len(shapes) == 1
    return pl.pallas_call(
        kernel,
        out_shape=shapes[0] if single else shapes,
        in_specs=in_specs,
        out_specs=out_specs[0] if single else out_specs,
        scratch_shapes=list(scratch),
        cost_estimate=pl.CostEstimate(flops=int(flops), bytes_accessed=moved, transcendentals=0),
        compiler_params=pltpu.CompilerParams(vmem_limit_bytes=limit),
    )(*args)


def exchange(cells):
    return lax.all_to_all(cells, "expert", split_axis=0, concat_axis=0, tiled=True)


def permute(x, pairs):
    return lax.ppermute(x, "fsdp", pairs)


def gather(shard, first, second):
    got = permute(shard, first)
    two = jnp.concatenate([shard, got], axis=0)
    other = permute(two, second)
    core_two = permute(two, PAIR_C)
    core_other = permute(other, PAIR_C)
    return two, other, core_two, core_other


def scatter(keep, send, unit):
    got = permute(send, PAIR_C)
    total = (keep.astype(F32) + got.astype(F32)).astype(BF16)
    half = total.shape[1] // 2
    left, right = total[:, :half], total[:, half:]
    got_l = permute(left[unit : 3 * unit], PAIR_A)
    got_r = permute(right[2 * unit :], PAIR_B)
    own_l = left[:unit].astype(F32) + got_l[:unit].astype(F32)
    next_l = left[3 * unit :].astype(F32) + got_l[unit:].astype(F32)
    own_r = right[:unit].astype(F32) + got_r[unit:].astype(F32)
    next_r = right[unit : 2 * unit].astype(F32) + got_r[:unit].astype(F32)
    got_l = permute(next_l.astype(BF16), PAIR_B)
    got_r = permute(next_r.astype(BF16), PAIR_A)
    return call(finish_kernel, [((unit, 2 * half), F32)], own_l, got_l, own_r, got_r, limit=16 << 20)


def layer(tokens, expert_ids, gate_weights, weight_in, weight_out, cotangent):
    n, width = tokens.shape
    experts = lax.axis_size("expert")
    cells = 4 * n
    capacity = cells // experts
    unit = weight_in.shape[1]
    in_pieces = gather(weight_in[0], PAIR_A, PAIR_B)
    out_pieces = gather(weight_out[0], PAIR_B, PAIR_A)

    anywhere = pl.BlockSpec(memory_space=pl.ANY)
    shape = (experts, 2 * capacity, width)
    sent = call(
        place_kernel,
        [(shape, BF16)],
        expert_ids.T,
        gate_weights.T,
        tokens,
        cotangent,
        specs=([anywhere] * 4, [anywhere]),
        scratch=[
            pltpu.VMEM((2, n), jnp.int32),
            pltpu.VMEM((2, n), F32),
            pltpu.VMEM(tokens.shape, BF16),
            pltpu.VMEM(tokens.shape, BF16),
            pltpu.VMEM(shape, BF16),
            pltpu.SemaphoreType.DMA((6,)),
        ],
    )
    rows = exchange(sent)
    place, hi, lo = call(
        functools.partial(weights_kernel, experts),
        [((n, cells), BF16)] * 3,
        expert_ids.T,
        gate_weights.T,
    )
    answer, hidden, grad_act = call(
        functools.partial(expert_kernel, unit),
        [(shape, BF16)] + [((cells, 8 * unit), BF16)] * 2,
        rows,
        *in_pieces,
        *out_pieces,
        flops=8 * cells * width * 8 * unit,
        moved=16 << 20,
        specs=([anywhere] * 9, [anywhere] * 3),
        scratch=[
            pltpu.VMEM(shape, BF16),
            pltpu.VMEM(shape, BF16),
            pltpu.VMEM((cells, 8 * unit), BF16),
            pltpu.VMEM((cells, 8 * unit), BF16),
            pltpu.VMEM((8 * unit, width), BF16),
            pltpu.VMEM((8 * unit, width), BF16),
            pltpu.SemaphoreType.DMA((2, 8)),
            pltpu.SemaphoreType.DMA((2,)),
            pltpu.SemaphoreType.DMA((2,)),
            pltpu.SemaphoreType.DMA((4,)),
        ],
    )
    returned = exchange(answer)

    grads = []
    for part, acts in ((1, hidden), (0, grad_act)):
        keep, send = call(
            functools.partial(grad_kernel, part, unit),
            [((4 * unit, width), BF16)] * 2,
            acts,
            rows,
            flops=2 * cells * width * 8 * unit,
            moved=8 << 20,
            scratch=[pltpu.VMEM((cells, width), BF16)],
        )
        grads.append(scatter(keep, send, unit))
    grad_out, grad_in = grads

    layer_out, token_grad = call(
        combine_kernel, [((n, width), BF16)] * 2, place, hi, lo, returned, limit=16 << 20
    )
    return (layer_out, token_grad, grad_in[None], grad_out[None])


def solution(mesh):
    rows = P(("fsdp", "expert"), None)
    weights = P("expert", "fsdp", None)
    return jax.shard_map(
        layer,
        mesh=mesh,
        in_specs=(rows, rows, rows, weights, weights, rows),
        out_specs=(rows, rows, weights, weights),
        check_vma=False,
    )
```

```python
import functools

import jax
import jax.numpy as jnp
from jax import lax
from jax.experimental import pallas as pl
from jax.experimental.pallas import tpu as pltpu
from jax.sharding import PartitionSpec as P


PAIR_A = [(2 * y + c, 2 * (y ^ 1) + c) for y in range(4) for c in range(2)]
PAIR_B = [(2 * y + c, 2 * (3 - y) + c) for y in range(4) for c in range(2)]
PAIR_C = [(f, f ^ 1) for f in range(8)]
F32 = jnp.float32
BF16 = jnp.bfloat16
GELU_SCALE = 0.7978845608028654
GELU_CUBIC = 0.044715


def dot_t(a, b):
    return lax.dot_general(a, b, (((1,), (1,)), ((), ())), preferred_element_type=F32)


def dot_0(a, b):
    return lax.dot_general(a, b, (((0,), (0,)), ((), ())), preferred_element_type=F32)


def dot(a, b):
    return jnp.dot(a, b, preferred_element_type=F32)


def cells_of(experts, capacity, ids_ref):
    n = ids_ref.shape[1]
    ids0, ids1 = ids_ref[0:1, :], ids_ref[1:2, :]
    label = lax.broadcasted_iota(jnp.int32, (experts, n), 0)
    oh0, oh1 = ids0 == label, ids1 == label
    hit = jnp.where(oh0 | oh1, 1.0, 0.0).astype(BF16)
    before = lax.broadcasted_iota(jnp.int32, (n, n), 0) < lax.broadcasted_iota(jnp.int32, (n, n), 1)
    earlier = dot(hit, jnp.where(before, 1.0, 0.0).astype(BF16))
    slot0 = jnp.sum(jnp.where(oh0, earlier, 0.0), axis=0, keepdims=True).astype(jnp.int32)
    slot1 = jnp.sum(jnp.where(oh1, earlier, 0.0), axis=0, keepdims=True).astype(jnp.int32)
    cell = lax.broadcasted_iota(jnp.int32, (experts * capacity, n), 0)
    return cell == ids0 * capacity + slot0, cell == ids1 * capacity + slot1


def place_kernel(*refs):
    hbm, out_hbm, local, cells_ref, sems = refs[:4], refs[4], refs[5:9], refs[9], refs[10]
    copies = [pltpu.make_async_copy(a, b, sems.at[i]) for i, (a, b) in enumerate(zip(hbm, local))]
    for copy in copies:
        copy.start()
    ids_ref, gate_ref, tok_ref, cot_ref = local
    experts, slots, width = cells_ref.shape
    capacity = slots // 2
    outs = [
        pltpu.make_async_copy(cells_ref.at[:, part, :], out_hbm.at[:, part, :], sems.at[4 + i])
        for i, part in enumerate((pl.ds(0, capacity), pl.ds(capacity, capacity)))
    ]
    copies[0].wait()
    at0, at1 = cells_of(experts, capacity, ids_ref)
    place = jnp.where(at0 | at1, 1.0, 0.0).astype(BF16)
    copies[2].wait()
    cells_ref[:, :capacity, :] = dot(place, tok_ref[...]).astype(BF16).reshape(experts, capacity, width)
    outs[0].start()
    copies[1].wait()
    gate = jnp.where(at0, gate_ref[0:1, :], 0.0) + jnp.where(at1, gate_ref[1:2, :], 0.0)
    hi = gate.astype(BF16)
    lo = (gate - hi.astype(F32)).astype(BF16)
    copies[3].wait()
    cot = cot_ref[...]
    cells_ref[:, capacity:, :] = (
        (dot(hi, cot) + dot(lo, cot)).astype(BF16).reshape(experts, capacity, width)
    )
    outs[1].start()
    outs[0].wait()
    outs[1].wait()


def weights_kernel(experts, ids_ref, gate_ref, place_ref, hi_ref, lo_ref):
    at0, at1 = cells_of(experts, place_ref.shape[1] // experts, ids_ref)
    place_ref[...] = jnp.transpose(jnp.where(at0 | at1, 1.0, 0.0)).astype(BF16)
    gate = jnp.where(at0, gate_ref[0:1, :], 0.0) + jnp.where(at1, gate_ref[1:2, :], 0.0)
    gate = jnp.transpose(gate)
    hi = gate.astype(BF16)
    hi_ref[...] = hi
    lo_ref[...] = (gate - hi.astype(F32)).astype(BF16)


def expert_kernel(unit, rows_hbm, *refs):
    in_a, in_b, in_ca, in_cb, out_a, out_b, out_ca, out_cb = refs[:8]
    back_hbm, hid_hbm, act_hbm = refs[8:11]
    rows_ref, back_ref, hid_ref, act_ref, full_in, full_out, sems, row_sem, out_sems, back_sems = refs[11:]
    sources, slots, width = rows_ref.shape
    capacity = slots // 2
    count = sources * capacity
    tile = count // 2
    per = sources // 2
    row_copies = [
        pltpu.make_async_copy(
            rows_hbm.at[pl.ds(r * per, per)], rows_ref.at[pl.ds(r * per, per)], row_sem.at[r]
        )
        for r in range(2)
    ]
    order = []
    for first, second, first_out, second_out in [(in_a, in_b, out_a, out_b), (in_ca, in_cb, out_ca, out_cb)]:
        order.append(((first, 0), (first_out, 0)))
        order.append(((first, 1), (second_out, 0)))
        order.append(((second, 1), (second_out, 1)))
        order.append(((second, 0), (first_out, 1)))

    def fetch(c):
        for w, ((ref, row), full) in enumerate(zip(order[c], (full_in, full_out))):
            pltpu.make_async_copy(
                ref.at[pl.ds(row * unit, unit)], full.at[pl.ds(c * unit, unit)], sems.at[w, c]
            ).start()

    for copy in row_copies:
        copy.start()
    fetch(0)
    for copy in row_copies:
        copy.wait()
    fetch(1)

    def act_copies(c, at):
        cut = pl.ds(at, unit)
        return [
            pltpu.make_async_copy(ref.at[:, cut], hbm.at[:, cut], out_sems.at[i, c])
            for i, (ref, hbm) in enumerate([(hid_ref, hid_hbm), (act_ref, act_hbm)])
        ]

    @pl.loop(0, 8)
    def _(c):
        for ahead in range(2, 8):

            @pl.when(c == ahead - 2)
            def _():
                fetch(ahead)

        at = pl.multiple_of(c * unit, unit)
        for w, full in enumerate((full_in, full_out)):
            pltpu.make_async_copy(in_a.at[pl.ds(0, unit)], full.at[pl.ds(at, unit)], sems.at[w, c]).wait()
        w_in, w_out = full_in[pl.ds(at, unit), :], full_out[pl.ds(at, unit), :]
        for r in range(2):
            x = rows_ref[r * per : (r + 1) * per, :capacity, :].reshape(tile, width)
            dy = rows_ref[r * per : (r + 1) * per, capacity:, :].reshape(tile, width)
            pre = dot_t(x, w_in)
            up = dot_t(dy, w_out)
            square = pre * pre
            half = 0.5 + 0.5 * jnp.tanh(pre * (GELU_SCALE + (GELU_SCALE * GELU_CUBIC) * square))
            hid = pre * half
            slope = half + hid * (1.0 - half) * (2.0 * GELU_SCALE + (6.0 * GELU_SCALE * GELU_CUBIC) * square)
            hid_ref[r * tile : (r + 1) * tile, pl.ds(at, unit)] = hid.astype(BF16)
            act_ref[r * tile : (r + 1) * tile, pl.ds(at, unit)] = (up * slope).astype(BF16)
        for copy in act_copies(c, at):
            copy.start()

    columns = 256

    def back_copy(c, at):
        cut = pl.ds(at, columns)
        return pltpu.make_async_copy(back_ref.at[:, :, cut], back_hbm.at[:, :, cut], back_sems.at[c])

    @pl.loop(0, width // columns)
    def _(c):
        at = pl.multiple_of(c * columns, columns)
        for part, (a_ref, full) in enumerate([(hid_ref, full_out), (act_ref, full_in)]):
            w = full[:, pl.ds(at, columns)]
            for r in range(2):
                got = dot(a_ref[r * tile : (r + 1) * tile, :], w).astype(BF16)
                back_ref[
                    r * per : (r + 1) * per, part * capacity : (part + 1) * capacity, pl.ds(at, columns)
                ] = got.reshape(per, capacity, columns)
        back_copy(c, at).start()

    for c in range(width // columns):
        back_copy(c, c * columns).wait()
    for c in range(8):
        for copy in act_copies(c, c * unit):
            copy.wait()


def grad_kernel(part, first, unit, acts_hbm, rows_hbm, out_hbm, acts_ref, rows_ref, out_ref, sems):
    width = out_ref.shape[1]
    sources, capacity, _ = rows_ref.shape
    chunks = out_ref.shape[0] // unit
    rows_copy = pltpu.make_async_copy(
        rows_hbm.at[:, pl.ds(part * capacity, capacity), :], rows_ref, sems.at[2 * chunks]
    )
    rows_copy.start()
    loads = [
        pltpu.make_async_copy(
            acts_hbm.at[:, pl.ds((first + c) * unit, unit)], acts_ref.at[c], sems.at[c]
        )
        for c in range(chunks)
    ]
    for load in loads:
        load.start()
    stores = [
        pltpu.make_async_copy(
            out_ref.at[pl.ds(c * unit, unit)], out_hbm.at[pl.ds(c * unit, unit)], sems.at[chunks + c]
        )
        for c in range(chunks)
    ]
    rows_copy.wait()
    rows = rows_ref[...].reshape(sources * capacity, width)
    for c in range(chunks):
        loads[c].wait()
        out_ref[c * unit : (c + 1) * unit, :] = dot_0(acts_ref[c], rows).astype(BF16)
        stores[c].start()
    for store in stores:
        store.wait()


def combine_kernel(place_ref, hi_ref, lo_ref, rows_ref, out_ref, grad_ref):
    sources, slots, width = rows_ref.shape
    capacity = slots // 2
    rows = rows_ref[:, :capacity, :].reshape(sources * capacity, width)
    out_ref[...] = (dot(hi_ref[...], rows) + dot(lo_ref[...], rows)).astype(BF16)
    rows = rows_ref[:, capacity:, :].reshape(sources * capacity, width)
    grad_ref[...] = dot(place_ref[...], rows).astype(BF16)


def finish_kernel(own_l_ref, got_l_ref, own_r_ref, got_r_ref, out_ref):
    half = own_l_ref.shape[1]
    out_ref[:, :half] = own_l_ref[...] + got_l_ref[...].astype(F32)
    out_ref[:, half:] = own_r_ref[...] + got_r_ref[...].astype(F32)


def call(kernel, outs, *args, flops=3e8, moved=4 << 20, specs=None, scratch=(), limit=None):
    shapes = [jax.ShapeDtypeStruct(s, d) for s, d in outs]
    vmem = pl.BlockSpec(memory_space=pltpu.VMEM)
    in_specs, out_specs = specs or ([vmem] * len(args), [vmem] * len(shapes))
    single = len(shapes) == 1
    return pl.pallas_call(
        kernel,
        out_shape=shapes[0] if single else shapes,
        in_specs=in_specs,
        out_specs=out_specs[0] if single else out_specs,
        scratch_shapes=list(scratch),
        cost_estimate=pl.CostEstimate(flops=int(flops), bytes_accessed=moved, transcendentals=0),
        compiler_params=pltpu.CompilerParams(vmem_limit_bytes=limit),
    )(*args)


def exchange(cells):
    return lax.all_to_all(cells, "expert", split_axis=0, concat_axis=0, tiled=True)


def permute(x, pairs):
    return lax.ppermute(x, "fsdp", pairs)


def gather(shard, first, second):
    got = permute(shard, first)
    two = jnp.concatenate([shard, got], axis=0)
    other = permute(two, second)
    core_two = permute(two, PAIR_C)
    core_other = permute(other, PAIR_C)
    return two, other, core_two, core_other


def scatter(keep, send, unit):
    got = permute(send, PAIR_C)
    total = (keep.astype(F32) + got.astype(F32)).astype(BF16)
    half = total.shape[1] // 2
    left, right = total[:, :half], total[:, half:]
    got_l = permute(left[unit : 3 * unit], PAIR_A)
    got_r = permute(right[2 * unit :], PAIR_B)
    own_l = left[:unit].astype(F32) + got_l[:unit].astype(F32)
    next_l = left[3 * unit :].astype(F32) + got_l[unit:].astype(F32)
    own_r = right[:unit].astype(F32) + got_r[unit:].astype(F32)
    next_r = right[unit : 2 * unit].astype(F32) + got_r[:unit].astype(F32)
    got_l = permute(next_l.astype(BF16), PAIR_B)
    got_r = permute(next_r.astype(BF16), PAIR_A)
    return call(finish_kernel, [((unit, 2 * half), F32)], own_l, got_l, own_r, got_r, limit=16 << 20)


def layer(tokens, expert_ids, gate_weights, weight_in, weight_out, cotangent):
    n, width = tokens.shape
    experts = lax.axis_size("expert")
    cells = 4 * n
    capacity = cells // experts
    unit = weight_in.shape[1]
    in_pieces = gather(weight_in[0], PAIR_A, PAIR_B)
    out_pieces = gather(weight_out[0], PAIR_B, PAIR_A)

    anywhere = pl.BlockSpec(memory_space=pl.ANY)
    shape = (experts, 2 * capacity, width)
    sent = call(
        place_kernel,
        [(shape, BF16)],
        expert_ids.T,
        gate_weights.T,
        tokens,
        cotangent,
        specs=([anywhere] * 4, [anywhere]),
        scratch=[
            pltpu.VMEM((2, n), jnp.int32),
            pltpu.VMEM((2, n), F32),
            pltpu.VMEM(tokens.shape, BF16),
            pltpu.VMEM(tokens.shape, BF16),
            pltpu.VMEM(shape, BF16),
            pltpu.SemaphoreType.DMA((6,)),
        ],
    )
    rows = exchange(sent)
    place, hi, lo = call(
        functools.partial(weights_kernel, experts),
        [((n, cells), BF16)] * 3,
        expert_ids.T,
        gate_weights.T,
    )
    answer, hidden, grad_act = call(
        functools.partial(expert_kernel, unit),
        [(shape, BF16)] + [((cells, 8 * unit), BF16)] * 2,
        rows,
        *in_pieces,
        *out_pieces,
        flops=8 * cells * width * 8 * unit,
        moved=16 << 20,
        specs=([anywhere] * 9, [anywhere] * 3),
        scratch=[
            pltpu.VMEM(shape, BF16),
            pltpu.VMEM(shape, BF16),
            pltpu.VMEM((cells, 8 * unit), BF16),
            pltpu.VMEM((cells, 8 * unit), BF16),
            pltpu.VMEM((8 * unit, width), BF16),
            pltpu.VMEM((8 * unit, width), BF16),
            pltpu.SemaphoreType.DMA((2, 8)),
            pltpu.SemaphoreType.DMA((2,)),
            pltpu.SemaphoreType.DMA((2, 8)),
            pltpu.SemaphoreType.DMA((4,)),
        ],
        limit=48 << 20,
    )
    returned = exchange(answer)

    grads = []
    for part, acts in ((1, hidden), (0, grad_act)):
        halves = []
        for first in (4, 0):
            halves.append(
                call(
                    functools.partial(grad_kernel, part, first, unit),
                    [((4 * unit, width), BF16)],
                    acts,
                    rows,
                    flops=cells * width * 8 * unit,
                    specs=([anywhere] * 2, [anywhere]),
                    scratch=[
                        pltpu.VMEM((4, cells, unit), BF16),
                        pltpu.VMEM((experts, capacity, width), BF16),
                        pltpu.VMEM((4 * unit, width), BF16),
                        pltpu.SemaphoreType.DMA((9,)),
                    ],
                )
            )
        send, keep = halves
        grads.append(scatter(keep, send, unit))
    grad_out, grad_in = grads

    layer_out, token_grad = call(
        combine_kernel, [((n, width), BF16)] * 2, place, hi, lo, returned, limit=16 << 20
    )
    return (layer_out, token_grad, grad_in[None], grad_out[None])


def solution(mesh):
    rows = P(("fsdp", "expert"), None)
    weights = P("expert", "fsdp", None)
    return jax.shard_map(
        layer,
        mesh=mesh,
        in_specs=(rows, rows, rows, weights, weights, rows),
        out_specs=(rows, rows, weights, weights),
        check_vma=False,
    )
```

```python
import functools

import jax
import jax.numpy as jnp
from jax import lax
from jax.experimental import pallas as pl
from jax.experimental.pallas import tpu as pltpu
from jax.sharding import PartitionSpec as P


PAIR_A = [(2 * y + c, 2 * (y ^ 1) + c) for y in range(4) for c in range(2)]
PAIR_B = [(2 * y + c, 2 * (3 - y) + c) for y in range(4) for c in range(2)]
PAIR_C = [(f, f ^ 1) for f in range(8)]
F32 = jnp.float32
BF16 = jnp.bfloat16
GELU_SCALE = 0.7978845608028654
GELU_CUBIC = 0.044715


def dot_t(a, b):
    return lax.dot_general(a, b, (((1,), (1,)), ((), ())), preferred_element_type=F32)


def dot(a, b):
    return jnp.dot(a, b, preferred_element_type=F32)


def cells_of(experts, capacity, ids_ref):
    n = ids_ref.shape[1]
    ids0, ids1 = ids_ref[0:1, :], ids_ref[1:2, :]
    label = lax.broadcasted_iota(jnp.int32, (experts, n), 0)
    oh0, oh1 = ids0 == label, ids1 == label
    hit = jnp.where(oh0 | oh1, 1.0, 0.0).astype(BF16)
    before = lax.broadcasted_iota(jnp.int32, (n, n), 0) < lax.broadcasted_iota(jnp.int32, (n, n), 1)
    earlier = dot(hit, jnp.where(before, 1.0, 0.0).astype(BF16))
    slot0 = jnp.sum(jnp.where(oh0, earlier, 0.0), axis=0, keepdims=True).astype(jnp.int32)
    slot1 = jnp.sum(jnp.where(oh1, earlier, 0.0), axis=0, keepdims=True).astype(jnp.int32)
    cell = lax.broadcasted_iota(jnp.int32, (experts * capacity, n), 0)
    return cell == ids0 * capacity + slot0, cell == ids1 * capacity + slot1


def place_kernel(*refs):
    hbm, out_hbm, local, cells_ref, sems = refs[:4], refs[4], refs[5:9], refs[9], refs[10]
    copies = [pltpu.make_async_copy(a, b, sems.at[i]) for i, (a, b) in enumerate(zip(hbm, local))]
    for copy in copies:
        copy.start()
    ids_ref, gate_ref, tok_ref, cot_ref = local
    experts, slots, width = cells_ref.shape
    capacity = slots // 2
    outs = [
        pltpu.make_async_copy(cells_ref.at[:, part, :], out_hbm.at[:, part, :], sems.at[4 + i])
        for i, part in enumerate((pl.ds(0, capacity), pl.ds(capacity, capacity)))
    ]
    copies[0].wait()
    at0, at1 = cells_of(experts, capacity, ids_ref)
    place = jnp.where(at0 | at1, 1.0, 0.0).astype(BF16)
    copies[2].wait()
    cells_ref[:, :capacity, :] = dot(place, tok_ref[...]).astype(BF16).reshape(experts, capacity, width)
    outs[0].start()
    copies[1].wait()
    gate = jnp.where(at0, gate_ref[0:1, :], 0.0) + jnp.where(at1, gate_ref[1:2, :], 0.0)
    hi = gate.astype(BF16)
    lo = (gate - hi.astype(F32)).astype(BF16)
    copies[3].wait()
    cot = cot_ref[...]
    cells_ref[:, capacity:, :] = (
        (dot(hi, cot) + dot(lo, cot)).astype(BF16).reshape(experts, capacity, width)
    )
    outs[1].start()
    outs[0].wait()
    outs[1].wait()


def weights_kernel(experts, ids_ref, gate_ref, place_ref, hi_ref, lo_ref):
    at0, at1 = cells_of(experts, place_ref.shape[1] // experts, ids_ref)
    place_ref[...] = jnp.transpose(jnp.where(at0 | at1, 1.0, 0.0)).astype(BF16)
    gate = jnp.where(at0, gate_ref[0:1, :], 0.0) + jnp.where(at1, gate_ref[1:2, :], 0.0)
    gate = jnp.transpose(gate)
    hi = gate.astype(BF16)
    hi_ref[...] = hi
    lo_ref[...] = (gate - hi.astype(F32)).astype(BF16)


def expert_kernel(unit, rows_hbm, *refs):
    in_a, in_b, in_ca, in_cb, out_a, out_b, out_ca, out_cb = refs[:8]
    back_hbm, hid_hbm, act_hbm = refs[8:11]
    rows_ref, back_ref, hid_ref, act_ref, full_in, full_out, sems, row_sem, out_sems, back_sems = refs[11:]
    sources, slots, width = rows_ref.shape
    capacity = slots // 2
    count = sources * capacity
    tile = count // 2
    per = sources // 2
    row_copies = [
        pltpu.make_async_copy(
            rows_hbm.at[pl.ds(r * per, per)], rows_ref.at[pl.ds(r * per, per)], row_sem.at[r]
        )
        for r in range(2)
    ]
    order = []
    for first, second, first_out, second_out in [(in_a, in_b, out_a, out_b), (in_ca, in_cb, out_ca, out_cb)]:
        order.append(((first, 0), (first_out, 0)))
        order.append(((first, 1), (second_out, 0)))
        order.append(((second, 1), (second_out, 1)))
        order.append(((second, 0), (first_out, 1)))

    def fetch(c):
        for w, ((ref, row), full) in enumerate(zip(order[c], (full_in, full_out))):
            pltpu.make_async_copy(
                ref.at[pl.ds(row * unit, unit)], full.at[pl.ds(c * unit, unit)], sems.at[w, c]
            ).start()

    for copy in row_copies:
        copy.start()
    fetch(0)
    for copy in row_copies:
        copy.wait()
    fetch(1)

    def act_copies(c, at):
        cut = pl.ds(at, unit)
        return [
            pltpu.make_async_copy(ref.at[:, cut], hbm.at[:, cut], out_sems.at[i, c])
            for i, (ref, hbm) in enumerate([(hid_ref, hid_hbm), (act_ref, act_hbm)])
        ]

    @pl.loop(0, 8)
    def _(c):
        for ahead in range(2, 8):

            @pl.when(c == ahead - 2)
            def _():
                fetch(ahead)

        at = pl.multiple_of(c * unit, unit)
        for w, full in enumerate((full_in, full_out)):
            pltpu.make_async_copy(in_a.at[pl.ds(0, unit)], full.at[pl.ds(at, unit)], sems.at[w, c]).wait()
        w_in, w_out = full_in[pl.ds(at, unit), :], full_out[pl.ds(at, unit), :]
        for r in range(2):
            x = rows_ref[r * per : (r + 1) * per, :capacity, :].reshape(tile, width)
            dy = rows_ref[r * per : (r + 1) * per, capacity:, :].reshape(tile, width)
            pre = dot_t(x, w_in)
            up = dot_t(dy, w_out)
            square = pre * pre
            half = 0.5 + 0.5 * jnp.tanh(pre * (GELU_SCALE + (GELU_SCALE * GELU_CUBIC) * square))
            hid = pre * half
            slope = half + hid * (1.0 - half) * (2.0 * GELU_SCALE + (6.0 * GELU_SCALE * GELU_CUBIC) * square)
            hid_ref[r * tile : (r + 1) * tile, pl.ds(at, unit)] = hid.astype(BF16)
            act_ref[r * tile : (r + 1) * tile, pl.ds(at, unit)] = (up * slope).astype(BF16)
        for copy in act_copies(c, at):
            copy.start()

    columns = 256

    def back_copy(c, at):
        cut = pl.ds(at, columns)
        return pltpu.make_async_copy(back_ref.at[:, :, cut], back_hbm.at[:, :, cut], back_sems.at[c])

    @pl.loop(0, width // columns)
    def _(c):
        at = pl.multiple_of(c * columns, columns)
        for part, (a_ref, full) in enumerate([(hid_ref, full_out), (act_ref, full_in)]):
            w = full[:, pl.ds(at, columns)]
            for r in range(2):
                got = dot(a_ref[r * tile : (r + 1) * tile, :], w).astype(BF16)
                back_ref[
                    r * per : (r + 1) * per, part * capacity : (part + 1) * capacity, pl.ds(at, columns)
                ] = got.reshape(per, capacity, columns)
        back_copy(c, at).start()

    for c in range(width // columns):
        back_copy(c, c * columns).wait()
    for c in range(8):
        for copy in act_copies(c, c * unit):
            copy.wait()


def grad_kernel(part, first, unit, acts_hbm, rows_hbm, *refs):
    last = first == 0
    if last:
        got_hbm, outs_hbm, (acts_ref, rows_ref, turned_ref, got_ref), outs, sems = (
            refs[0], refs[1:6], refs[6:10], refs[10:15], refs[15]
        )
    else:
        outs_hbm, (acts_ref, rows_ref, turned_ref), outs, sems = refs[:1], refs[1:4], refs[4:5], refs[5]
    sources, capacity, width = rows_ref.shape
    columns = 256
    chunks = width // columns
    copies = [
        pltpu.make_async_copy(acts_hbm.at[:, pl.ds(first * unit, 4 * unit)], acts_ref, sems.at[0]),
        pltpu.make_async_copy(rows_hbm.at[:, pl.ds(part * capacity, capacity), :], rows_ref, sems.at[1]),
    ]
    if last:
        copies.append(pltpu.make_async_copy(got_hbm, got_ref, sems.at[2]))
    for copy in copies:
        copy.start()
    copies[0].wait()
    for c in range(4):
        turned_ref[c * unit : (c + 1) * unit, :] = jnp.transpose(acts_ref[:, c * unit : (c + 1) * unit])
    for copy in copies[1:]:
        copy.wait()
    stores = []

    def store(at, ref, hbm):
        stores.append(pltpu.make_async_copy(ref, hbm, sems.at[at]))
        stores[-1].start()

    for c in range(chunks):
        cut = slice(c * columns, (c + 1) * columns)
        rows = rows_ref[:, :, cut].reshape(sources * capacity, columns)
        got = dot(turned_ref[...], rows)
        if not last:
            outs[0][:, cut] = got.astype(BF16)
            window = pl.ds(c * columns, columns)
            store(3 + c, outs[0].at[:, window], outs_hbm[0].at[:, window])
            continue
        got = got + got_ref[:, cut].astype(F32)
        own_ref, left_ref, right_ref, next_l_ref, next_r_ref = outs
        own_ref[:, cut] = got[:unit]
        side = slice((c % (chunks // 2)) * columns, (c % (chunks // 2) + 1) * columns)
        if c < chunks // 2:
            left_ref[:, side] = got[unit : 3 * unit].astype(BF16)
            next_l_ref[:, side] = got[3 * unit :]
        else:
            right_ref[:, side] = got[2 * unit :].astype(BF16)
            next_r_ref[:, side] = got[unit : 2 * unit]
        if c == chunks // 2 - 1:
            store(3, left_ref, outs_hbm[1])
            store(4, next_l_ref, outs_hbm[3])
    if last:
        store(5, right_ref, outs_hbm[2])
        store(6, next_r_ref, outs_hbm[4])
        store(7, own_ref, outs_hbm[0])
    for copy in stores:
        copy.wait()


def combine_kernel(place_ref, hi_ref, lo_ref, rows_ref, out_ref, grad_ref):
    sources, slots, width = rows_ref.shape
    capacity = slots // 2
    rows = rows_ref[:, :capacity, :].reshape(sources * capacity, width)
    out_ref[...] = (dot(hi_ref[...], rows) + dot(lo_ref[...], rows)).astype(BF16)
    rows = rows_ref[:, capacity:, :].reshape(sources * capacity, width)
    grad_ref[...] = dot(place_ref[...], rows).astype(BF16)


def finish_kernel(own_ref, first_l_ref, got_l_ref, first_r_ref, got_r_ref, out_ref):
    half = got_l_ref.shape[1]
    unit = out_ref.shape[0]
    out_ref[:, :half] = own_ref[:, :half] + first_l_ref[:unit, :].astype(F32) + got_l_ref[...].astype(F32)
    out_ref[:, half:] = own_ref[:, half:] + first_r_ref[unit:, :].astype(F32) + got_r_ref[...].astype(F32)


def call(kernel, outs, *args, flops=3e8, moved=4 << 20, specs=None, scratch=(), limit=None):
    shapes = [jax.ShapeDtypeStruct(s, d) for s, d in outs]
    vmem = pl.BlockSpec(memory_space=pltpu.VMEM)
    in_specs, out_specs = specs or ([vmem] * len(args), [vmem] * len(shapes))
    single = len(shapes) == 1
    return pl.pallas_call(
        kernel,
        out_shape=shapes[0] if single else shapes,
        in_specs=in_specs,
        out_specs=out_specs[0] if single else out_specs,
        scratch_shapes=list(scratch),
        cost_estimate=pl.CostEstimate(flops=int(flops), bytes_accessed=moved, transcendentals=0),
        compiler_params=pltpu.CompilerParams(vmem_limit_bytes=limit),
    )(*args)


def exchange(cells):
    return lax.all_to_all(cells, "expert", split_axis=0, concat_axis=0, tiled=True)


def permute(x, pairs):
    return lax.ppermute(x, "fsdp", pairs)


def gather(shard, first, second):
    got = permute(shard, first)
    two = jnp.concatenate([shard, got], axis=0)
    other = permute(two, second)
    core_two = permute(two, PAIR_C)
    core_other = permute(other, PAIR_C)
    return two, other, core_two, core_other


def scatter(acts, rows, part, unit):
    cells = acts.shape[0]
    sources, slots, width = rows.shape
    anywhere = pl.BlockSpec(memory_space=pl.ANY)

    def product(first, outs, *more):
        return call(
            functools.partial(grad_kernel, part, first, unit),
            outs,
            acts,
            rows,
            *more,
            flops=cells * width * 8 * unit,
            specs=([anywhere] * (2 + len(more)), [anywhere] * len(outs)),
            scratch=[
                pltpu.VMEM((cells, 4 * unit), BF16),
                pltpu.VMEM((sources, slots // 2, width), BF16),
                pltpu.VMEM((4 * unit, cells), BF16),
            ]
            + [pltpu.VMEM(m.shape, m.dtype) for m in more]
            + [pltpu.VMEM(s, d) for s, d in outs]
            + [pltpu.SemaphoreType.DMA((8,))],
        )

    half = width // 2
    send = product(4, [((4 * unit, width), BF16)])
    got = permute(send, PAIR_C)
    own, left, right, next_l, next_r = product(
        0,
        [((unit, width), F32)] + [((2 * unit, half), BF16)] * 2 + [((unit, half), F32)] * 2,
        got,
    )
    first_l = permute(left, PAIR_A)
    first_r = permute(right, PAIR_B)
    next_l = (next_l + first_l[unit:].astype(F32)).astype(BF16)
    next_r = (next_r + first_r[:unit].astype(F32)).astype(BF16)
    got_l = permute(next_l, PAIR_B)
    got_r = permute(next_r, PAIR_A)
    return call(
        finish_kernel, [((unit, width), F32)], own, first_l, got_l, first_r, got_r, limit=16 << 20
    )


def layer(tokens, expert_ids, gate_weights, weight_in, weight_out, cotangent):
    n, width = tokens.shape
    experts = lax.axis_size("expert")
    cells = 4 * n
    capacity = cells // experts
    unit = weight_in.shape[1]
    in_pieces = gather(weight_in[0], PAIR_A, PAIR_B)
    out_pieces = gather(weight_out[0], PAIR_B, PAIR_A)

    anywhere = pl.BlockSpec(memory_space=pl.ANY)
    shape = (experts, 2 * capacity, width)
    sent = call(
        place_kernel,
        [(shape, BF16)],
        expert_ids.T,
        gate_weights.T,
        tokens,
        cotangent,
        specs=([anywhere] * 4, [anywhere]),
        scratch=[
            pltpu.VMEM((2, n), jnp.int32),
            pltpu.VMEM((2, n), F32),
            pltpu.VMEM(tokens.shape, BF16),
            pltpu.VMEM(tokens.shape, BF16),
            pltpu.VMEM(shape, BF16),
            pltpu.SemaphoreType.DMA((6,)),
        ],
    )
    rows = exchange(sent)
    place, hi, lo = call(
        functools.partial(weights_kernel, experts),
        [((n, cells), BF16)] * 3,
        expert_ids.T,
        gate_weights.T,
    )
    answer, hidden, grad_act = call(
        functools.partial(expert_kernel, unit),
        [(shape, BF16)] + [((cells, 8 * unit), BF16)] * 2,
        rows,
        *in_pieces,
        *out_pieces,
        flops=8 * cells * width * 8 * unit,
        moved=16 << 20,
        specs=([anywhere] * 9, [anywhere] * 3),
        scratch=[
            pltpu.VMEM(shape, BF16),
            pltpu.VMEM(shape, BF16),
            pltpu.VMEM((cells, 8 * unit), BF16),
            pltpu.VMEM((cells, 8 * unit), BF16),
            pltpu.VMEM((8 * unit, width), BF16),
            pltpu.VMEM((8 * unit, width), BF16),
            pltpu.SemaphoreType.DMA((2, 8)),
            pltpu.SemaphoreType.DMA((2,)),
            pltpu.SemaphoreType.DMA((2, 8)),
            pltpu.SemaphoreType.DMA((4,)),
        ],
        limit=48 << 20,
    )
    returned = exchange(answer)

    grad_out = scatter(hidden, rows, 1, unit)
    grad_in = scatter(grad_act, rows, 0, unit)

    layer_out, token_grad = call(
        combine_kernel, [((n, width), BF16)] * 2, place, hi, lo, returned, limit=16 << 20
    )
    return (layer_out, token_grad, grad_in[None], grad_out[None])


def solution(mesh):
    rows = P(("fsdp", "expert"), None)
    weights = P("expert", "fsdp", None)
    return jax.shard_map(
        layer,
        mesh=mesh,
        in_specs=(rows, rows, rows, weights, weights, rows),
        out_specs=(rows, rows, weights, weights),
        check_vma=False,
    )
```

```python
import functools

import jax
import jax.numpy as jnp
from jax import lax
from jax.experimental import pallas as pl
from jax.experimental.pallas import tpu as pltpu
from jax.sharding import PartitionSpec as P


PAIR_A = [(2 * y + c, 2 * (y ^ 1) + c) for y in range(4) for c in range(2)]
PAIR_B = [(2 * y + c, 2 * (3 - y) + c) for y in range(4) for c in range(2)]
PAIR_C = [(f, f ^ 1) for f in range(8)]
F32 = jnp.float32
BF16 = jnp.bfloat16
GELU_SCALE = 0.7978845608028654
GELU_CUBIC = 0.044715


def dot_t(a, b):
    return lax.dot_general(a, b, (((1,), (1,)), ((), ())), preferred_element_type=F32)


def dot_0(a, b):
    return lax.dot_general(a, b, (((0,), (0,)), ((), ())), preferred_element_type=F32)


def dot(a, b):
    return jnp.dot(a, b, preferred_element_type=F32)


def cells_of(experts, capacity, ids_ref):
    n = ids_ref.shape[1]
    ids0, ids1 = ids_ref[0:1, :], ids_ref[1:2, :]
    label = lax.broadcasted_iota(jnp.int32, (experts, n), 0)
    oh0, oh1 = ids0 == label, ids1 == label
    hit = jnp.where(oh0 | oh1, 1.0, 0.0).astype(BF16)
    before = lax.broadcasted_iota(jnp.int32, (n, n), 0) < lax.broadcasted_iota(jnp.int32, (n, n), 1)
    earlier = dot(hit, jnp.where(before, 1.0, 0.0).astype(BF16))
    slot0 = jnp.sum(jnp.where(oh0, earlier, 0.0), axis=0, keepdims=True).astype(jnp.int32)
    slot1 = jnp.sum(jnp.where(oh1, earlier, 0.0), axis=0, keepdims=True).astype(jnp.int32)
    cell = lax.broadcasted_iota(jnp.int32, (experts * capacity, n), 0)
    return cell == ids0 * capacity + slot0, cell == ids1 * capacity + slot1


def place_kernel(*refs):
    hbm, out_hbm, local, cells_ref, sems = refs[:4], refs[4], refs[5:9], refs[9], refs[10]
    copies = [pltpu.make_async_copy(a, b, sems.at[i]) for i, (a, b) in enumerate(zip(hbm, local))]
    for copy in copies:
        copy.start()
    ids_ref, gate_ref, tok_ref, cot_ref = local
    experts, slots, width = cells_ref.shape
    capacity = slots // 2
    outs = [
        pltpu.make_async_copy(cells_ref.at[:, part, :], out_hbm.at[:, part, :], sems.at[4 + i])
        for i, part in enumerate((pl.ds(0, capacity), pl.ds(capacity, capacity)))
    ]
    copies[0].wait()
    at0, at1 = cells_of(experts, capacity, ids_ref)
    place = jnp.where(at0 | at1, 1.0, 0.0).astype(BF16)
    copies[2].wait()
    cells_ref[:, :capacity, :] = dot(place, tok_ref[...]).astype(BF16).reshape(experts, capacity, width)
    outs[0].start()
    copies[1].wait()
    gate = jnp.where(at0, gate_ref[0:1, :], 0.0) + jnp.where(at1, gate_ref[1:2, :], 0.0)
    hi = gate.astype(BF16)
    lo = (gate - hi.astype(F32)).astype(BF16)
    copies[3].wait()
    cot = cot_ref[...]
    cells_ref[:, capacity:, :] = (
        (dot(hi, cot) + dot(lo, cot)).astype(BF16).reshape(experts, capacity, width)
    )
    outs[1].start()
    outs[0].wait()
    outs[1].wait()


def weights_kernel(experts, ids_ref, gate_ref, place_ref, hi_ref, lo_ref):
    at0, at1 = cells_of(experts, place_ref.shape[1] // experts, ids_ref)
    place_ref[...] = jnp.transpose(jnp.where(at0 | at1, 1.0, 0.0)).astype(BF16)
    gate = jnp.where(at0, gate_ref[0:1, :], 0.0) + jnp.where(at1, gate_ref[1:2, :], 0.0)
    gate = jnp.transpose(gate)
    hi = gate.astype(BF16)
    hi_ref[...] = hi
    lo_ref[...] = (gate - hi.astype(F32)).astype(BF16)


def expert_kernel(unit, rows_hbm, *refs):
    in_a, in_b, in_ca, in_cb, out_a, out_b, out_ca, out_cb = refs[:8]
    back_hbm, hid_hbm, act_hbm, send_out_hbm, send_in_hbm = refs[8:13]
    rows_ref, back_ref, hid_ref, act_ref, send_out_ref, send_in_ref, full_in, full_out = refs[13:21]
    sems, row_sem, out_sems, send_sems, back_sems = refs[21:]
    sources, slots, width = rows_ref.shape
    capacity = slots // 2
    count = sources * capacity
    tile = count // 2
    per = sources // 2
    row_copies = [
        pltpu.make_async_copy(
            rows_hbm.at[pl.ds(r * per, per)], rows_ref.at[pl.ds(r * per, per)], row_sem.at[r]
        )
        for r in range(2)
    ]
    order = []
    for first, second, first_out, second_out in [(in_a, in_b, out_a, out_b), (in_ca, in_cb, out_ca, out_cb)]:
        order.append(((first, 0), (first_out, 0)))
        order.append(((first, 1), (second_out, 0)))
        order.append(((second, 1), (second_out, 1)))
        order.append(((second, 0), (first_out, 1)))

    def fetch(c):
        for w, ((ref, row), full) in enumerate(zip(order[c], (full_in, full_out))):
            pltpu.make_async_copy(
                ref.at[pl.ds(row * unit, unit)], full.at[pl.ds(c * unit, unit)], sems.at[w, c]
            ).start()

    for copy in row_copies:
        copy.start()
    fetch(0)
    for copy in row_copies:
        copy.wait()
    fetch(1)

    def act_copies(c, at):
        cut = pl.ds(at, unit)
        return [
            pltpu.make_async_copy(ref.at[:, cut], hbm.at[:, cut], out_sems.at[i, c])
            for i, (ref, hbm) in enumerate([(hid_ref, hid_hbm), (act_ref, act_hbm)])
        ]

    @pl.loop(0, 8)
    def _(c):
        for ahead in range(2, 8):

            @pl.when(c == ahead - 2)
            def _():
                fetch(ahead)

        at = pl.multiple_of(c * unit, unit)
        for w, full in enumerate((full_in, full_out)):
            pltpu.make_async_copy(in_a.at[pl.ds(0, unit)], full.at[pl.ds(at, unit)], sems.at[w, c]).wait()
        w_in, w_out = full_in[pl.ds(at, unit), :], full_out[pl.ds(at, unit), :]
        for r in range(2):
            x = rows_ref[r * per : (r + 1) * per, :capacity, :].reshape(tile, width)
            dy = rows_ref[r * per : (r + 1) * per, capacity:, :].reshape(tile, width)
            pre = dot_t(x, w_in)
            up = dot_t(dy, w_out)
            square = pre * pre
            half = 0.5 + 0.5 * jnp.tanh(pre * (GELU_SCALE + (GELU_SCALE * GELU_CUBIC) * square))
            hid = pre * half
            slope = half + hid * (1.0 - half) * (2.0 * GELU_SCALE + (6.0 * GELU_SCALE * GELU_CUBIC) * square)
            hid_ref[r * tile : (r + 1) * tile, pl.ds(at, unit)] = hid.astype(BF16)
            act_ref[r * tile : (r + 1) * tile, pl.ds(at, unit)] = (up * slope).astype(BF16)

        @pl.when(c < 4)
        def _():
            for copy in act_copies(c, at):
                copy.start()

    columns = 256
    sends = [(1, hid_ref, send_out_ref, send_out_hbm), (0, act_ref, send_in_ref, send_in_hbm)]

    def send_copy(i, c, at):
        cut = pl.ds(at, columns)
        return pltpu.make_async_copy(sends[i][2].at[:, cut], sends[i][3].at[:, cut], send_sems.at[i, c])

    @pl.loop(0, width // columns)
    def _(c):
        at = pl.multiple_of(c * columns, columns)
        for i, (part, a_ref, ref, _) in enumerate(sends):
            rows = rows_ref[:, part * capacity : (part + 1) * capacity, pl.ds(at, columns)]
            got = dot_0(a_ref[:, 4 * unit :], rows.reshape(count, columns))
            ref[:, pl.ds(at, columns)] = got.astype(BF16)
            send_copy(i, c, at).start()

    def back_copy(c, at):
        cut = pl.ds(at, columns)
        return pltpu.make_async_copy(back_ref.at[:, :, cut], back_hbm.at[:, :, cut], back_sems.at[c])

    @pl.loop(0, width // columns)
    def _(c):
        at = pl.multiple_of(c * columns, columns)
        for part, (a_ref, full) in enumerate([(hid_ref, full_out), (act_ref, full_in)]):
            w = full[:, pl.ds(at, columns)]
            for r in range(2):
                got = dot(a_ref[r * tile : (r + 1) * tile, :], w).astype(BF16)
                back_ref[
                    r * per : (r + 1) * per, part * capacity : (part + 1) * capacity, pl.ds(at, columns)
                ] = got.reshape(per, capacity, columns)
        back_copy(c, at).start()

    for c in range(width // columns):
        back_copy(c, c * columns).wait()
    for c in range(4):
        for copy in act_copies(c, c * unit):
            copy.wait()
    for c in range(width // columns):
        for i in range(2):
            send_copy(i, c, c * columns).wait()


def grad_kernel(part, unit, acts_hbm, rows_hbm, got_hbm, *refs):
    outs_hbm, (acts_ref, rows_ref, got_ref), outs, sems = refs[:5], refs[5:8], refs[8:13], refs[13]
    sources, capacity, width = rows_ref.shape
    columns = 256
    chunks = width // columns
    copies = [
        pltpu.make_async_copy(acts_hbm, acts_ref, sems.at[0]),
        pltpu.make_async_copy(rows_hbm.at[:, pl.ds(part * capacity, capacity), :], rows_ref, sems.at[1]),
        pltpu.make_async_copy(got_hbm, got_ref, sems.at[2]),
    ]
    for copy in copies:
        copy.start()
    for copy in copies:
        copy.wait()
    stores = []

    def store(at, ref, hbm):
        stores.append(pltpu.make_async_copy(ref, hbm, sems.at[at]))
        stores[-1].start()

    own_ref, left_ref, right_ref, next_l_ref, next_r_ref = outs
    for c in range(chunks):
        cut = slice(c * columns, (c + 1) * columns)
        got = dot_0(acts_ref[...], rows_ref[:, :, cut].reshape(sources * capacity, columns))
        got = got + got_ref[:, cut].astype(F32)
        own_ref[:, cut] = got[:unit]
        side = slice((c % (chunks // 2)) * columns, (c % (chunks // 2) + 1) * columns)
        if c < chunks // 2:
            left_ref[:, side] = got[unit : 3 * unit].astype(BF16)
            next_l_ref[:, side] = got[3 * unit :]
        else:
            right_ref[:, side] = got[2 * unit :].astype(BF16)
            next_r_ref[:, side] = got[unit : 2 * unit]
        if c == chunks // 2 - 1:
            store(3, left_ref, outs_hbm[1])
            store(4, next_l_ref, outs_hbm[3])
    store(5, right_ref, outs_hbm[2])
    store(6, next_r_ref, outs_hbm[4])
    store(7, own_ref, outs_hbm[0])
    for copy in stores:
        copy.wait()


def combine_kernel(place_ref, hi_ref, lo_ref, rows_ref, out_ref, grad_ref):
    sources, slots, width = rows_ref.shape
    capacity = slots // 2
    rows = rows_ref[:, :capacity, :].reshape(sources * capacity, width)
    out_ref[...] = (dot(hi_ref[...], rows) + dot(lo_ref[...], rows)).astype(BF16)
    rows = rows_ref[:, capacity:, :].reshape(sources * capacity, width)
    grad_ref[...] = dot(place_ref[...], rows).astype(BF16)


def finish_kernel(own_ref, first_l_ref, got_l_ref, first_r_ref, got_r_ref, out_ref):
    half = got_l_ref.shape[1]
    unit = out_ref.shape[0]
    out_ref[:, :half] = own_ref[:, :half] + first_l_ref[:unit, :].astype(F32) + got_l_ref[...].astype(F32)
    out_ref[:, half:] = own_ref[:, half:] + first_r_ref[unit:, :].astype(F32) + got_r_ref[...].astype(F32)


def call(kernel, outs, *args, flops=3e8, moved=4 << 20, specs=None, scratch=(), limit=None):
    shapes = [jax.ShapeDtypeStruct(s, d) for s, d in outs]
    vmem = pl.BlockSpec(memory_space=pltpu.VMEM)
    in_specs, out_specs = specs or ([vmem] * len(args), [vmem] * len(shapes))
    single = len(shapes) == 1
    return pl.pallas_call(
        kernel,
        out_shape=shapes[0] if single else shapes,
        in_specs=in_specs,
        out_specs=out_specs[0] if single else out_specs,
        scratch_shapes=list(scratch),
        cost_estimate=pl.CostEstimate(flops=int(flops), bytes_accessed=moved, transcendentals=0),
        compiler_params=pltpu.CompilerParams(vmem_limit_bytes=limit),
    )(*args)


def exchange(cells):
    return lax.all_to_all(cells, "expert", split_axis=0, concat_axis=0, tiled=True)


def permute(x, pairs):
    return lax.ppermute(x, "fsdp", pairs)


def gather(shard, first, second):
    got = permute(shard, first)
    two = jnp.concatenate([shard, got], axis=0)
    other = permute(two, second)
    core_two = permute(two, PAIR_C)
    core_other = permute(other, PAIR_C)
    return two, other, core_two, core_other


def scatter(send, acts, rows, part, unit):
    cells = acts.shape[0]
    sources, slots, width = rows.shape
    half = width // 2
    anywhere = pl.BlockSpec(memory_space=pl.ANY)
    outs = [((unit, width), F32)] + [((2 * unit, half), BF16)] * 2 + [((unit, half), F32)] * 2
    got = permute(send, PAIR_C)
    own, left, right, next_l, next_r = call(
        functools.partial(grad_kernel, part, unit),
        outs,
        acts,
        rows,
        got,
        flops=cells * width * 8 * unit,
        specs=([anywhere] * 3, [anywhere] * 5),
        scratch=[
            pltpu.VMEM(acts.shape, BF16),
            pltpu.VMEM((sources, slots // 2, width), BF16),
            pltpu.VMEM(got.shape, BF16),
        ]
        + [pltpu.VMEM(s, d) for s, d in outs]
        + [pltpu.SemaphoreType.DMA((8,))],
    )
    first_l = permute(left, PAIR_A)
    first_r = permute(right, PAIR_B)
    next_l = (next_l + first_l[unit:].astype(F32)).astype(BF16)
    next_r = (next_r + first_r[:unit].astype(F32)).astype(BF16)
    got_l = permute(next_l, PAIR_B)
    got_r = permute(next_r, PAIR_A)
    return call(
        finish_kernel, [((unit, width), F32)], own, first_l, got_l, first_r, got_r, limit=16 << 20
    )


def layer(tokens, expert_ids, gate_weights, weight_in, weight_out, cotangent):
    n, width = tokens.shape
    experts = lax.axis_size("expert")
    cells = 4 * n
    capacity = cells // experts
    unit = weight_in.shape[1]
    in_pieces = gather(weight_in[0], PAIR_A, PAIR_B)
    out_pieces = gather(weight_out[0], PAIR_B, PAIR_A)

    anywhere = pl.BlockSpec(memory_space=pl.ANY)
    shape = (experts, 2 * capacity, width)
    sent = call(
        place_kernel,
        [(shape, BF16)],
        expert_ids.T,
        gate_weights.T,
        tokens,
        cotangent,
        specs=([anywhere] * 4, [anywhere]),
        scratch=[
            pltpu.VMEM((2, n), jnp.int32),
            pltpu.VMEM((2, n), F32),
            pltpu.VMEM(tokens.shape, BF16),
            pltpu.VMEM(tokens.shape, BF16),
            pltpu.VMEM(shape, BF16),
            pltpu.SemaphoreType.DMA((6,)),
        ],
    )
    rows = exchange(sent)
    place, hi, lo = call(
        functools.partial(weights_kernel, experts),
        [((n, cells), BF16)] * 3,
        expert_ids.T,
        gate_weights.T,
    )
    answer, hidden, grad_act, send_out, send_in = call(
        functools.partial(expert_kernel, unit),
        [(shape, BF16)] + [((cells, 4 * unit), BF16)] * 2 + [((4 * unit, width), BF16)] * 2,
        rows,
        *in_pieces,
        *out_pieces,
        flops=10 * cells * width * 8 * unit,
        moved=16 << 20,
        specs=([anywhere] * 9, [anywhere] * 5),
        scratch=[
            pltpu.VMEM(shape, BF16),
            pltpu.VMEM(shape, BF16),
            pltpu.VMEM((cells, 8 * unit), BF16),
            pltpu.VMEM((cells, 8 * unit), BF16),
            pltpu.VMEM((4 * unit, width), BF16),
            pltpu.VMEM((4 * unit, width), BF16),
            pltpu.VMEM((8 * unit, width), BF16),
            pltpu.VMEM((8 * unit, width), BF16),
            pltpu.SemaphoreType.DMA((2, 8)),
            pltpu.SemaphoreType.DMA((2,)),
            pltpu.SemaphoreType.DMA((2, 4)),
            pltpu.SemaphoreType.DMA((2, 4)),
            pltpu.SemaphoreType.DMA((4,)),
        ],
        limit=48 << 20,
    )
    returned = exchange(answer)

    grad_out = scatter(send_out, hidden, rows, 1, unit)
    grad_in = scatter(send_in, grad_act, rows, 0, unit)

    layer_out, token_grad = call(
        combine_kernel, [((n, width), BF16)] * 2, place, hi, lo, returned, limit=16 << 20
    )
    return (layer_out, token_grad, grad_in[None], grad_out[None])


def solution(mesh):
    rows = P(("fsdp", "expert"), None)
    weights = P("expert", "fsdp", None)
    return jax.shard_map(
        layer,
        mesh=mesh,
        in_specs=(rows, rows, rows, weights, weights, rows),
        out_specs=(rows, rows, weights, weights),
        check_vma=False,
    )
```

```python
import functools

import jax
import jax.numpy as jnp
from jax import lax
from jax.experimental import pallas as pl
from jax.experimental.pallas import tpu as pltpu
from jax.sharding import PartitionSpec as P


PAIR_A = [(2 * y + c, 2 * (y ^ 1) + c) for y in range(4) for c in range(2)]
PAIR_B = [(2 * y + c, 2 * (3 - y) + c) for y in range(4) for c in range(2)]
PAIR_C = [(f, f ^ 1) for f in range(8)]
F32 = jnp.float32
BF16 = jnp.bfloat16
GELU_SCALE = 0.7978845608028654
GELU_CUBIC = 0.044715


def dot_t(a, b):
    return lax.dot_general(a, b, (((1,), (1,)), ((), ())), preferred_element_type=F32)


def dot_0(a, b):
    return lax.dot_general(a, b, (((0,), (0,)), ((), ())), preferred_element_type=F32)


def dot(a, b):
    return jnp.dot(a, b, preferred_element_type=F32)


def cells_of(experts, capacity, ids_ref):
    n = ids_ref.shape[1]
    ids0, ids1 = ids_ref[0:1, :], ids_ref[1:2, :]
    label = lax.broadcasted_iota(jnp.int32, (experts, n), 0)
    oh0, oh1 = ids0 == label, ids1 == label
    hit = jnp.where(oh0 | oh1, 1.0, 0.0).astype(BF16)
    before = lax.broadcasted_iota(jnp.int32, (n, n), 0) < lax.broadcasted_iota(jnp.int32, (n, n), 1)
    earlier = dot(hit, jnp.where(before, 1.0, 0.0).astype(BF16))
    slot0 = jnp.sum(jnp.where(oh0, earlier, 0.0), axis=0, keepdims=True).astype(jnp.int32)
    slot1 = jnp.sum(jnp.where(oh1, earlier, 0.0), axis=0, keepdims=True).astype(jnp.int32)
    cell = lax.broadcasted_iota(jnp.int32, (experts * capacity, n), 0)
    return cell == ids0 * capacity + slot0, cell == ids1 * capacity + slot1


def place_kernel(*refs):
    hbm, out_hbm, local, cells_ref, sems = refs[:4], refs[4], refs[5:9], refs[9], refs[10]
    copies = [pltpu.make_async_copy(a, b, sems.at[i]) for i, (a, b) in enumerate(zip(hbm, local))]
    for copy in copies:
        copy.start()
    ids_ref, gate_ref, tok_ref, cot_ref = local
    experts, slots, width = cells_ref.shape
    capacity = slots // 2
    outs = [
        pltpu.make_async_copy(cells_ref.at[:, part, :], out_hbm.at[:, part, :], sems.at[4 + i])
        for i, part in enumerate((pl.ds(0, capacity), pl.ds(capacity, capacity)))
    ]
    copies[0].wait()
    at0, at1 = cells_of(experts, capacity, ids_ref)
    place = jnp.where(at0 | at1, 1.0, 0.0).astype(BF16)
    copies[2].wait()
    cells_ref[:, :capacity, :] = dot(place, tok_ref[...]).astype(BF16).reshape(experts, capacity, width)
    outs[0].start()
    copies[1].wait()
    gate = jnp.where(at0, gate_ref[0:1, :], 0.0) + jnp.where(at1, gate_ref[1:2, :], 0.0)
    hi = gate.astype(BF16)
    lo = (gate - hi.astype(F32)).astype(BF16)
    copies[3].wait()
    cot = cot_ref[...]
    cells_ref[:, capacity:, :] = (
        (dot(hi, cot) + dot(lo, cot)).astype(BF16).reshape(experts, capacity, width)
    )
    outs[1].start()
    outs[0].wait()
    outs[1].wait()


def weights_kernel(experts, ids_ref, gate_ref, place_ref, hi_ref, lo_ref):
    at0, at1 = cells_of(experts, place_ref.shape[1] // experts, ids_ref)
    place_ref[...] = jnp.transpose(jnp.where(at0 | at1, 1.0, 0.0)).astype(BF16)
    gate = jnp.where(at0, gate_ref[0:1, :], 0.0) + jnp.where(at1, gate_ref[1:2, :], 0.0)
    gate = jnp.transpose(gate)
    hi = gate.astype(BF16)
    hi_ref[...] = hi
    lo_ref[...] = (gate - hi.astype(F32)).astype(BF16)


def expert_kernel(unit, rows_hbm, *refs):
    in_a, in_b, in_ca, in_cb, out_a, out_b, out_ca, out_cb = refs[:8]
    back_hbm, hid_hbm, act_hbm, send_hbm = refs[8:12]
    rows_ref, back_ref, hid_ref, act_ref, send_ref, full_in, full_out = refs[12:19]
    sems, row_sem, out_sems, send_sems, back_sems = refs[19:]
    sources, slots, width = rows_ref.shape
    capacity = slots // 2
    count = sources * capacity
    tile = count // 2
    per = sources // 2
    row_copies = [
        pltpu.make_async_copy(
            rows_hbm.at[pl.ds(r * per, per)], rows_ref.at[pl.ds(r * per, per)], row_sem.at[r]
        )
        for r in range(2)
    ]
    order = []
    for first, second, first_out, second_out in [(in_a, in_b, out_a, out_b), (in_ca, in_cb, out_ca, out_cb)]:
        order.append(((first, 0), (first_out, 0)))
        order.append(((first, 1), (second_out, 0)))
        order.append(((second, 1), (second_out, 1)))
        order.append(((second, 0), (first_out, 1)))

    def fetch(c):
        for w, ((ref, row), full) in enumerate(zip(order[c], (full_in, full_out))):
            pltpu.make_async_copy(
                ref.at[pl.ds(row * unit, unit)], full.at[pl.ds(c * unit, unit)], sems.at[w, c]
            ).start()

    for copy in row_copies:
        copy.start()
    fetch(0)
    for copy in row_copies:
        copy.wait()
    fetch(1)

    def act_copies(c, at):
        cut = pl.ds(at, unit)
        return [
            pltpu.make_async_copy(ref.at[:, cut], hbm.at[:, cut], out_sems.at[i, c])
            for i, (ref, hbm) in enumerate([(hid_ref, hid_hbm), (act_ref, act_hbm)])
        ]

    @pl.loop(0, 8)
    def _(c):
        for ahead in range(2, 8):

            @pl.when(c == ahead - 2)
            def _():
                fetch(ahead)

        at = pl.multiple_of(c * unit, unit)
        for w, full in enumerate((full_in, full_out)):
            pltpu.make_async_copy(in_a.at[pl.ds(0, unit)], full.at[pl.ds(at, unit)], sems.at[w, c]).wait()
        w_in, w_out = full_in[pl.ds(at, unit), :], full_out[pl.ds(at, unit), :]
        for r in range(2):
            x = rows_ref[r * per : (r + 1) * per, :capacity, :].reshape(tile, width)
            dy = rows_ref[r * per : (r + 1) * per, capacity:, :].reshape(tile, width)
            pre = dot_t(x, w_in)
            up = dot_t(dy, w_out)
            square = pre * pre
            half = 0.5 + 0.5 * jnp.tanh(pre * (GELU_SCALE + (GELU_SCALE * GELU_CUBIC) * square))
            hid = pre * half
            slope = half + hid * (1.0 - half) * (2.0 * GELU_SCALE + (6.0 * GELU_SCALE * GELU_CUBIC) * square)
            hid_ref[r * tile : (r + 1) * tile, pl.ds(at, unit)] = hid.astype(BF16)
            act_ref[r * tile : (r + 1) * tile, pl.ds(at, unit)] = (up * slope).astype(BF16)
        for copy in act_copies(c, at):
            copy.start()

    columns = 256

    def send_copy(c, at):
        cut = pl.ds(at, columns)
        return pltpu.make_async_copy(send_ref.at[:, cut], send_hbm.at[:, cut], send_sems.at[c])

    @pl.loop(0, width // columns)
    def _(c):
        at = pl.multiple_of(c * columns, columns)
        rows = rows_ref[:, capacity:, pl.ds(at, columns)].reshape(count, columns)
        send_ref[:, pl.ds(at, columns)] = dot_0(hid_ref[:, 4 * unit :], rows).astype(BF16)
        send_copy(c, at).start()

    def back_copy(c, at):
        cut = pl.ds(at, columns)
        return pltpu.make_async_copy(back_ref.at[:, :, cut], back_hbm.at[:, :, cut], back_sems.at[c])

    @pl.loop(0, width // columns)
    def _(c):
        at = pl.multiple_of(c * columns, columns)
        for part, (a_ref, full) in enumerate([(hid_ref, full_out), (act_ref, full_in)]):
            w = full[:, pl.ds(at, columns)]
            for r in range(2):
                got = dot(a_ref[r * tile : (r + 1) * tile, :], w).astype(BF16)
                back_ref[
                    r * per : (r + 1) * per, part * capacity : (part + 1) * capacity, pl.ds(at, columns)
                ] = got.reshape(per, capacity, columns)
        back_copy(c, at).start()

    for c in range(width // columns):
        back_copy(c, c * columns).wait()
    for c in range(8):
        for copy in act_copies(c, c * unit):
            copy.wait()
    for c in range(width // columns):
        send_copy(c, c * columns).wait()


def grad_kernel(part, first, unit, acts_hbm, rows_hbm, *refs):
    last = first == 0
    if last:
        got_hbm, outs_hbm, (acts_ref, rows_ref, turned_ref, got_ref), outs, sems = (
            refs[0], refs[1:6], refs[6:10], refs[10:15], refs[15]
        )
    else:
        outs_hbm, (acts_ref, rows_ref, turned_ref), outs, sems = refs[:1], refs[1:4], refs[4:5], refs[5]
    sources, capacity, width = rows_ref.shape
    columns = 256
    chunks = width // columns
    copies = [
        pltpu.make_async_copy(acts_hbm.at[:, pl.ds(first * unit, 4 * unit)], acts_ref, sems.at[0]),
        pltpu.make_async_copy(rows_hbm.at[:, pl.ds(part * capacity, capacity), :], rows_ref, sems.at[1]),
    ]
    if last:
        copies.append(pltpu.make_async_copy(got_hbm, got_ref, sems.at[2]))
    for copy in copies:
        copy.start()
    copies[0].wait()
    for c in range(4):
        turned_ref[c * unit : (c + 1) * unit, :] = jnp.transpose(acts_ref[:, c * unit : (c + 1) * unit])
    for copy in copies[1:]:
        copy.wait()
    stores = []

    def store(at, ref, hbm):
        stores.append(pltpu.make_async_copy(ref, hbm, sems.at[at]))
        stores[-1].start()

    for c in range(chunks):
        cut = slice(c * columns, (c + 1) * columns)
        rows = rows_ref[:, :, cut].reshape(sources * capacity, columns)
        got = dot(turned_ref[...], rows)
        if not last:
            outs[0][:, cut] = got.astype(BF16)
            window = pl.ds(c * columns, columns)
            store(3 + c, outs[0].at[:, window], outs_hbm[0].at[:, window])
            continue
        got = got + got_ref[:, cut].astype(F32)
        own_ref, left_ref, right_ref, next_l_ref, next_r_ref = outs
        own_ref[:, cut] = got[:unit]
        side = slice((c % (chunks // 2)) * columns, (c % (chunks // 2) + 1) * columns)
        if c < chunks // 2:
            left_ref[:, side] = got[unit : 3 * unit].astype(BF16)
            next_l_ref[:, side] = got[3 * unit :]
        else:
            right_ref[:, side] = got[2 * unit :].astype(BF16)
            next_r_ref[:, side] = got[unit : 2 * unit]
        if c == chunks // 2 - 1:
            store(3, left_ref, outs_hbm[1])
            store(4, next_l_ref, outs_hbm[3])
    if last:
        store(5, right_ref, outs_hbm[2])
        store(6, next_r_ref, outs_hbm[4])
        store(7, own_ref, outs_hbm[0])
    for copy in stores:
        copy.wait()


def combine_kernel(place_ref, hi_ref, lo_ref, rows_ref, out_ref, grad_ref):
    sources, slots, width = rows_ref.shape
    capacity = slots // 2
    rows = rows_ref[:, :capacity, :].reshape(sources * capacity, width)
    out_ref[...] = (dot(hi_ref[...], rows) + dot(lo_ref[...], rows)).astype(BF16)
    rows = rows_ref[:, capacity:, :].reshape(sources * capacity, width)
    grad_ref[...] = dot(place_ref[...], rows).astype(BF16)


def finish_kernel(own_ref, first_l_ref, got_l_ref, first_r_ref, got_r_ref, out_ref):
    half = got_l_ref.shape[1]
    unit = out_ref.shape[0]
    out_ref[:, :half] = own_ref[:, :half] + first_l_ref[:unit, :].astype(F32) + got_l_ref[...].astype(F32)
    out_ref[:, half:] = own_ref[:, half:] + first_r_ref[unit:, :].astype(F32) + got_r_ref[...].astype(F32)


def call(kernel, outs, *args, flops=3e8, moved=4 << 20, specs=None, scratch=(), limit=None):
    shapes = [jax.ShapeDtypeStruct(s, d) for s, d in outs]
    vmem = pl.BlockSpec(memory_space=pltpu.VMEM)
    in_specs, out_specs = specs or ([vmem] * len(args), [vmem] * len(shapes))
    single = len(shapes) == 1
    return pl.pallas_call(
        kernel,
        out_shape=shapes[0] if single else shapes,
        in_specs=in_specs,
        out_specs=out_specs[0] if single else out_specs,
        scratch_shapes=list(scratch),
        cost_estimate=pl.CostEstimate(flops=int(flops), bytes_accessed=moved, transcendentals=0),
        compiler_params=pltpu.CompilerParams(vmem_limit_bytes=limit),
    )(*args)


def exchange(cells):
    return lax.all_to_all(cells, "expert", split_axis=0, concat_axis=0, tiled=True)


def permute(x, pairs):
    return lax.ppermute(x, "fsdp", pairs)


def gather(shard, first, second):
    got = permute(shard, first)
    two = jnp.concatenate([shard, got], axis=0)
    other = permute(two, second)
    core_two = permute(two, PAIR_C)
    core_other = permute(other, PAIR_C)
    return two, other, core_two, core_other


def scatter(send, acts, rows, part, unit):
    cells = acts.shape[0]
    sources, slots, width = rows.shape
    anywhere = pl.BlockSpec(memory_space=pl.ANY)

    def product(first, outs, *more):
        return call(
            functools.partial(grad_kernel, part, first, unit),
            outs,
            acts,
            rows,
            *more,
            flops=cells * width * 8 * unit,
            specs=([anywhere] * (2 + len(more)), [anywhere] * len(outs)),
            scratch=[
                pltpu.VMEM((cells, 4 * unit), BF16),
                pltpu.VMEM((sources, slots // 2, width), BF16),
                pltpu.VMEM((4 * unit, cells), BF16),
            ]
            + [pltpu.VMEM(m.shape, m.dtype) for m in more]
            + [pltpu.VMEM(s, d) for s, d in outs]
            + [pltpu.SemaphoreType.DMA((8,))],
        )

    half = width // 2
    if send is None:
        send = product(4, [((4 * unit, width), BF16)])
    got = permute(send, PAIR_C)
    own, left, right, next_l, next_r = product(
        0,
        [((unit, width), F32)] + [((2 * unit, half), BF16)] * 2 + [((unit, half), F32)] * 2,
        got,
    )
    first_l = permute(left, PAIR_A)
    first_r = permute(right, PAIR_B)
    next_l = (next_l + first_l[unit:].astype(F32)).astype(BF16)
    next_r = (next_r + first_r[:unit].astype(F32)).astype(BF16)
    got_l = permute(next_l, PAIR_B)
    got_r = permute(next_r, PAIR_A)
    return call(
        finish_kernel, [((unit, width), F32)], own, first_l, got_l, first_r, got_r, limit=16 << 20
    )


def layer(tokens, expert_ids, gate_weights, weight_in, weight_out, cotangent):
    n, width = tokens.shape
    experts = lax.axis_size("expert")
    cells = 4 * n
    capacity = cells // experts
    unit = weight_in.shape[1]
    in_pieces = gather(weight_in[0], PAIR_A, PAIR_B)
    out_pieces = gather(weight_out[0], PAIR_B, PAIR_A)

    anywhere = pl.BlockSpec(memory_space=pl.ANY)
    shape = (experts, 2 * capacity, width)
    sent = call(
        place_kernel,
        [(shape, BF16)],
        expert_ids.T,
        gate_weights.T,
        tokens,
        cotangent,
        specs=([anywhere] * 4, [anywhere]),
        scratch=[
            pltpu.VMEM((2, n), jnp.int32),
            pltpu.VMEM((2, n), F32),
            pltpu.VMEM(tokens.shape, BF16),
            pltpu.VMEM(tokens.shape, BF16),
            pltpu.VMEM(shape, BF16),
            pltpu.SemaphoreType.DMA((6,)),
        ],
    )
    rows = exchange(sent)
    place, hi, lo = call(
        functools.partial(weights_kernel, experts),
        [((n, cells), BF16)] * 3,
        expert_ids.T,
        gate_weights.T,
        limit=16 << 20,
    )
    answer, hidden, grad_act, send_out = call(
        functools.partial(expert_kernel, unit),
        [(shape, BF16)] + [((cells, 8 * unit), BF16)] * 2 + [((4 * unit, width), BF16)],
        rows,
        *in_pieces,
        *out_pieces,
        flops=9 * cells * width * 8 * unit,
        moved=16 << 20,
        specs=([anywhere] * 9, [anywhere] * 4),
        scratch=[
            pltpu.VMEM(shape, BF16),
            pltpu.VMEM(shape, BF16),
            pltpu.VMEM((cells, 8 * unit), BF16),
            pltpu.VMEM((cells, 8 * unit), BF16),
            pltpu.VMEM((4 * unit, width), BF16),
            pltpu.VMEM((8 * unit, width), BF16),
            pltpu.VMEM((8 * unit, width), BF16),
            pltpu.SemaphoreType.DMA((2, 8)),
            pltpu.SemaphoreType.DMA((2,)),
            pltpu.SemaphoreType.DMA((2, 8)),
            pltpu.SemaphoreType.DMA((4,)),
            pltpu.SemaphoreType.DMA((4,)),
        ],
        limit=48 << 20,
    )
    returned = exchange(answer)

    grad_out = scatter(send_out, hidden, rows, 1, unit)
    grad_in = scatter(None, grad_act, rows, 0, unit)

    layer_out, token_grad = call(
        combine_kernel, [((n, width), BF16)] * 2, place, hi, lo, returned, limit=16 << 20
    )
    return (layer_out, token_grad, grad_in[None], grad_out[None])


def solution(mesh):
    rows = P(("fsdp", "expert"), None)
    weights = P("expert", "fsdp", None)
    return jax.shard_map(
        layer,
        mesh=mesh,
        in_specs=(rows, rows, rows, weights, weights, rows),
        out_specs=(rows, rows, weights, weights),
        check_vma=False,
    )
```
